32 devices in a mesh: clips: 2 (over x), frames: 8 (over z, y), heads: 2 (over core).
Axes of the slice: x: 2, y: 2, z: 4, core: 2. Of those that a mesh axis runs over, the one named last changes fastest.
Arguments:
- tokens: bfloat16 [16, 16, 56, 576], P(('clips', 'frames'), None, None, 'heads'), parts along dimension 0, may hold values from -6 to 6
- out_grad: bfloat16 [16, 16, 56, 576], P(('clips', 'frames'), None, None, 'heads'), parts along dimension 0, may hold values from -6 to 6
- w_qkv: bfloat16 [3, 576, 576], P(None, None, 'heads'), may hold values from -0.25 to 0.25
- pool_kernel: float32 [2, 27, 576], P(None, None, 'heads'), may hold values from -1.25 to 1.25
Outputs:
- input_grad: bfloat16 [16, 16, 56, 576], P(('clips', 'frames'), None, None, 'heads'), parts along dimension 0
- weight_grad: float32 [6, 576, 576], P('clips', 'frames', 'heads'), parts along dimension 0
- kernel_grad: float32 [4, 27, 576], P('clips', None, 'heads'), parts along dimension 0
The draws below stay inside these ranges and needn't reach their ends.
There are 2 independent parts, one for each index of `clips`. The reference program is written for one: setup_inputs(seed, part) draws one part's arguments, and reference() takes and returns one part's arrays. A program takes and returns all parts, laid end to end along the dimension named above; an argument that names none is the same for every part. Nothing has to cross between parts.
All inputs are finite; a program needn't handle non-finite values.
Results may differ from the reference program's by a relative error of at most 0.023.
Values may be sent and summed in bfloat16 or wider, within the bound.
No kernel may reach another device: no remote copies, remote signals or barrier semaphores. Data moves between devices by JAX's collectives and lax.ppermute only.
A program may use at most 64 MiB of HBM per device.

```python
import jax
import jax.numpy as jnp
from jax import lax

D = 576
HEADS = 8
ROWS = 16
COLS = 56
FRAMES = 8


def block_levels(stream_key, shape, shards, smallest, high):
    def one(dim, blocks):
        steps = jax.random.uniform(jax.random.fold_in(jax.random.fold_in(stream_key, 6), dim), (blocks,), jnp.float32, smallest / len(shards), high / len(shards))
        return jnp.repeat(jnp.exp(steps), shape[dim] // blocks).reshape((-1,) + (1,) * (len(shape) - dim - 1))

    factor_of = one(*shards[0])
    for cut in shards[1:]:
        factor_of = factor_of * one(*cut)
    return factor_of


def scatter_about(rng, dims, spread, bound, split=(), held_as=jnp.bfloat16):
    array = jax.random.normal(rng, dims, jnp.float32) * spread
    if len(split) > 0:
        array = block_levels(rng, dims, split, -0.22, 0.18) * array
    return jnp.clip(array, min=-bound, max=bound).astype(held_as)


def setup_inputs(seed: int = 0, part: int = 0) -> dict:
    key_of = jax.random.split(jax.random.key(seed), 5)
    part_splits = jax.random.split(jax.random.fold_in(key_of[4], part), 5)
    tokens = scatter_about(part_splits[0], (FRAMES, ROWS, COLS, D), 1.0, 6.0, ((0, 8), (3, 2)))
    out_grad = scatter_about(part_splits[1], (FRAMES, ROWS, COLS, D), 1.0, 6.0, ((0, 8), (3, 2)))
    w_qkv = scatter_about(key_of[2], (3, D, D), D ** -0.5, 0.25, ((2, 2),))
    pool_kernel = scatter_about(key_of[3], (2, 27, D), 27 ** -0.5, 1.25, ((2, 2),), jnp.float32)
    return dict(tokens=tokens, out_grad=out_grad, w_qkv=w_qkv, pool_kernel=pool_kernel)


def pool_grid(field, kernel):
    channels = field.shape[-1]
    taps = kernel.reshape(3, 3, 3, 1, channels)
    pooled = lax.conv_general_dilated(field[None], taps, (1, 4, 4), ((1, 1), (1, 1), (1, 1)), dimension_numbers=('NDHWC', 'DHWIO', 'NDHWC'), feature_group_count=channels, precision=lax.Precision.HIGHEST)
    return pooled[0]

def pool_pair(key_grid, value_grid, kernel):
    return (pool_grid(key_grid, kernel[0]), pool_grid(value_grid, kernel[1]))

def lowered(field):
    return lax.optimization_barrier(field.astype(jnp.bfloat16)).astype(jnp.float32)

def reference(tokens, out_grad, w_qkv, pool_kernel):
    frame_count, row_count, col_count, channels = tokens.shape
    head_dim = channels // HEADS
    scale = head_dim ** (-0.5)
    flat = tokens.reshape(-1, channels)
    queries = jnp.dot(flat, w_qkv[0], preferred_element_type=jnp.float32).astype(jnp.bfloat16)
    keys_full = jnp.dot(flat, w_qkv[1], preferred_element_type=jnp.float32).astype(jnp.bfloat16)
    values_full = jnp.dot(flat, w_qkv[2], preferred_element_type=jnp.float32).astype(jnp.bfloat16)
    grid = (frame_count, row_count, col_count, channels)
    (key_pool, value_pool), pull_back = jax.vjp(pool_pair, keys_full.reshape(grid).astype(jnp.float32), values_full.reshape(grid).astype(jnp.float32), pool_kernel)
    key_heads = lowered(key_pool).reshape(-1, HEADS, head_dim)
    value_heads = lowered(value_pool).reshape(-1, HEADS, head_dim)
    key_total = key_heads.shape[0]
    query_frames = queries.reshape(frame_count, row_count * col_count, HEADS, head_dim)
    grad_frames = out_grad.reshape(frame_count, row_count * col_count, HEADS, head_dim)

    def one_frame(carry, item):
        query_part, grad_part = item
        query_wide = query_part.astype(jnp.float32)
        grad_wide = grad_part.astype(jnp.float32)
        scores = jnp.einsum('qhd,khd->hqk', query_wide, key_heads) * scale
        raised = jnp.exp(scores)
        probs = raised / lax.optimization_barrier(jnp.sum(raised, axis=-1, keepdims=True))
        probs_low = lowered(probs)
        prob_grad = jnp.einsum('qhd,khd->hqk', grad_wide, value_heads)
        centre = lax.optimization_barrier(jnp.sum(probs * prob_grad, axis=-1, keepdims=True))
        score_grad = lowered(probs * (prob_grad - centre) * scale)
        query_grad = (grad_wide + jnp.einsum('hqk,khd->qhd', score_grad, key_heads)).astype(jnp.bfloat16)
        key_acc = carry[0] + jnp.einsum('hqk,qhd->khd', score_grad, query_wide)
        value_acc = carry[1] + jnp.einsum('hqk,qhd->khd', probs_low, grad_wide)
        return ((key_acc, value_acc), query_grad)
    start = (jnp.zeros((key_total, HEADS, head_dim), jnp.float32), jnp.zeros((key_total, HEADS, head_dim), jnp.float32))
    (key_sum, value_sum), query_grads = lax.scan(one_frame, start, (query_frames, grad_frames))
    key_tan, value_tan, kernel_grad = pull_back((key_sum.reshape(key_pool.shape), value_sum.reshape(value_pool.shape)))
    query_back = query_grads.reshape(-1, channels)
    key_back = key_tan.astype(jnp.bfloat16).reshape(-1, channels)
    value_back = value_tan.astype(jnp.bfloat16).reshape(-1, channels)
    input_sum = jnp.dot(query_back, w_qkv[0].T, preferred_element_type=jnp.float32)
    input_sum = input_sum + jnp.dot(key_back, w_qkv[1].T, preferred_element_type=jnp.float32)
    input_sum = input_sum + jnp.dot(value_back, w_qkv[2].T, preferred_element_type=jnp.float32)
    input_grad = input_sum.astype(jnp.bfloat16).reshape(tokens.shape)
    weight_grad = jnp.stack([jnp.dot(flat.T, query_back, preferred_element_type=jnp.float32), jnp.dot(flat.T, key_back, preferred_element_type=jnp.float32), jnp.dot(flat.T, value_back, preferred_element_type=jnp.float32)])
    return (input_grad, weight_grad, kernel_grad.astype(jnp.float32))
```

```python
import jax
import jax.numpy as jnp
from jax import lax
from jax.sharding import PartitionSpec as P

HEADS = 8


def as_sent(array):

    def short(part):
        return part.astype(jnp.bfloat16) if part.dtype == jnp.float32 else part

    return jax.tree.map(short, array)


def from_behind(value, axis, steps):
    count = lax.axis_size(axis)
    leading, last = (max(0, -steps), min(count, count - steps))
    return lax.ppermute(value, axis, [(source, source + steps) for source in range(leading, last)])


def with_halo(array, sides, width):
    for axis, dim in sides:
        count, length = (lax.axis_size(axis), array.shape[dim])
        up = [(i, (i + 1) % count) for i in range(count - 1)]
        down = [(j, i) for i, j in up]
        last = lax.slice_in_dim(array, length - width, length, axis=dim)
        leading = lax.slice_in_dim(array, 0, width, axis=dim)
        before = lax.ppermute(last, axis, up)
        after = lax.ppermute(leading, axis, down)
        array = jnp.concatenate([before, array, after], axis=dim)
    return array


def frame_pairs(step, flip):
    count = lax.axis_size("frames")
    return [(i, i ^ (2 * step + flip)) for i in range(count)]


def gather_frames(block):
    outer = lax.axis_size("frames") // 2
    same = [block] + [lax.ppermute(block, "frames", frame_pairs(s, 0)) for s in range(1, outer)]
    other = lax.ppermute(jnp.concatenate(same), "frames", frame_pairs(0, 1))
    return jnp.concatenate(same + [other])


def scatter_frames(terms):
    outer = lax.axis_size("frames") // 2
    half = terms.shape[0] // 2
    moved = lax.ppermute(terms[half:].astype(jnp.bfloat16), "frames", frame_pairs(0, 1))
    summed = terms[:half].astype(jnp.float32) + moved.astype(jnp.float32)
    blocks = summed.reshape(outer, half // outer, *terms.shape[1:])
    low = blocks.astype(jnp.bfloat16)
    own = blocks[0]
    for step in range(1, outer):
        own = own + lax.ppermute(low[step], "frames", frame_pairs(step, 0)).astype(jnp.float32)
    return own


def scatter_weights(terms, kernel_part):
    count = lax.axis_size("frames")
    outer = count // 2
    rows, width = terms.shape[0] // count, terms.shape[1]
    place = lax.axis_index("frames")
    low = terms.astype(jnp.bfloat16).reshape(count, rows, width)

    def block(relative):
        return lax.dynamic_index_in_dim(low, place ^ relative, 0, False)

    extra = kernel_part.reshape(-1, width)
    away = [block(2 * step + 1) for step in range(outer)] + [extra.astype(jnp.bfloat16)]
    moved = lax.ppermute(jnp.concatenate(away), "frames", frame_pairs(0, 1)).astype(jnp.float32)
    here = jnp.concatenate([block(2 * step).astype(jnp.float32) for step in range(outer)] + [extra])
    summed = here + moved
    tail = summed[outer * rows :]
    own = jnp.concatenate([summed[:rows], tail])
    for step in range(1, outer):
        piece = jnp.concatenate([summed[step * rows : (step + 1) * rows], tail]).astype(jnp.bfloat16)
        own = own + lax.ppermute(piece, "frames", frame_pairs(step, 0)).astype(jnp.float32)
    return own[:rows], own[rows:].reshape(kernel_part.shape)


def spatial_pool(frame, kernel_nine):
    channels = frame.shape[-1]
    taps = kernel_nine.reshape(3, 3, 1, channels)
    pooled = lax.conv_general_dilated(
        frame[None],
        taps,
        (4, 4),
        ((1, 1), (1, 1)),
        dimension_numbers=("NHWC", "HWIO", "NHWC"),
        feature_group_count=channels,
        precision=lax.Precision.HIGHEST,
    )
    return pooled[0]


def head_backward(scale):

    def run_head(item):
        query_head, grad_head, key_head, value_head = item
        scores = (
            jnp.einsum("qd,kd->qk", query_head, key_head, preferred_element_type=jnp.float32)
            * scale
        )
        raised = jnp.exp(scores)
        probs = raised / jnp.sum(raised, axis=-1, keepdims=True)
        probs_low = probs.astype(jnp.bfloat16)
        prob_grad = jnp.einsum(
            "qd,kd->qk", grad_head, value_head, preferred_element_type=jnp.float32
        )
        centre = jnp.sum(probs * prob_grad, axis=-1, keepdims=True)
        score_grad = (probs * (prob_grad - centre) * scale).astype(jnp.bfloat16)
        query_grad = (
            grad_head.astype(jnp.float32)
            + jnp.dot(score_grad, key_head, preferred_element_type=jnp.float32)
        ).astype(jnp.bfloat16)
        key_grad = jnp.einsum(
            "qk,qd->kd", score_grad, query_head, preferred_element_type=jnp.float32
        )
        value_grad = jnp.einsum(
            "qk,qd->kd", probs_low, grad_head, preferred_element_type=jnp.float32
        )
        return (query_grad, key_grad, value_grad)

    return run_head


def shards(tokens, out_grad, w_qkv, pool_kernel):
    local = tokens.shape[-1]
    heads_here = HEADS // lax.axis_size("heads")
    head_dim = local // heads_here
    scale = head_dim ** (-0.5)
    row_count = tokens.shape[1]
    col_count = tokens.shape[2]
    pooled_rows = row_count // 4
    pooled_cols = col_count // 4
    token_count = row_count * col_count
    whole = lax.all_gather(tokens, "heads", axis=3, tiled=True)
    flat = whole.reshape(token_count, -1)
    queries = jnp.dot(flat, w_qkv[0], preferred_element_type=jnp.float32).astype(jnp.bfloat16)
    key_proj = jnp.dot(flat, w_qkv[1], preferred_element_type=jnp.float32).astype(jnp.bfloat16)
    value_proj = jnp.dot(flat, w_qkv[2], preferred_element_type=jnp.float32).astype(jnp.bfloat16)
    own_frame = jnp.concatenate([key_proj, value_proj], axis=1).reshape(
        row_count, col_count, 2 * local
    )
    own_wide = own_frame.astype(jnp.float32)
    kernel_both = jnp.concatenate([pool_kernel[0], pool_kernel[1]], axis=1)
    earlier = spatial_pool(own_wide, kernel_both[0:9])
    middle = spatial_pool(own_wide, kernel_both[9:18])
    later = spatial_pool(own_wide, kernel_both[18:27])
    pooled = (
        from_behind(as_sent(earlier), "frames", 1).astype(earlier.dtype)
        + middle
        + from_behind(later, "frames", -1)
    )
    pooled_low = pooled.astype(jnp.bfloat16).reshape(pooled_rows * pooled_cols, 2 * local)
    all_keys = gather_frames(pooled_low)
    key_count = all_keys.shape[0]
    key_heads = all_keys[:, :local].reshape(key_count, heads_here, head_dim).transpose(1, 0, 2)
    value_heads = all_keys[:, local:].reshape(key_count, heads_here, head_dim).transpose(1, 0, 2)
    query_heads = queries.reshape(token_count, heads_here, head_dim).transpose(1, 0, 2)
    grad_heads = out_grad.reshape(token_count, heads_here, head_dim).transpose(1, 0, 2)
    query_parts, key_parts, value_parts = lax.map(
        head_backward(scale), (query_heads, grad_heads, key_heads, value_heads)
    )
    query_back = query_parts.transpose(1, 0, 2).reshape(token_count, local)
    key_terms = jnp.concatenate(
        [
            key_parts.transpose(1, 0, 2).reshape(key_count, local),
            value_parts.transpose(1, 0, 2).reshape(key_count, local),
        ],
        axis=1,
    )
    owned = scatter_frames(key_terms)
    window_grad = with_halo(
        owned.reshape(1, pooled_rows, pooled_cols, 2 * local).astype(jnp.bfloat16),
        (("frames", 0),),
        1,
    ).astype(jnp.float32)
    frame_grad = jnp.zeros((row_count, col_count, 2 * local), jnp.float32)
    kernel_parts = []
    for offset in range(3):
        unused, pull_back = jax.vjp(
            spatial_pool, own_wide, kernel_both[9 * offset : 9 * offset + 9]
        )
        part_frame, part_kernel = pull_back(window_grad[2 - offset])
        frame_grad = frame_grad + part_frame
        kernel_parts.append(part_kernel)
    kernel_local = jnp.concatenate(kernel_parts, axis=0)
    kernel_part = jnp.stack([kernel_local[:, :local], kernel_local[:, local:]])
    back_low = frame_grad.astype(jnp.bfloat16).reshape(token_count, 2 * local)
    grads = jnp.stack([query_back, back_low[:, :local], back_low[:, local:]])
    weight_terms = jnp.einsum("tc,itd->cid", flat, grads, preferred_element_type=jnp.float32)
    weight_part, kernel_grad = scatter_weights(weight_terms.reshape(-1, 3 * local), kernel_part)
    weight_grad = weight_part.reshape(-1, 3, local).transpose(1, 0, 2)
    summed = lax.psum_scatter(
        jnp.einsum("icd,itd->ct", w_qkv, grads, preferred_element_type=jnp.float32).astype(
            jnp.bfloat16
        ),
        "heads",
        scatter_dimension=0,
        tiled=True,
    ).astype(jnp.float32)
    input_grad = summed.T.astype(jnp.bfloat16).reshape(tokens.shape)
    return (input_grad, weight_grad, kernel_grad)


def solution(mesh):
    in_specs = (
        P(("clips", "frames"), None, None, "heads"),
        P(("clips", "frames"), None, None, "heads"),
        P(None, None, "heads"),
        P(None, None, "heads"),
    )
    out_specs = (
        P(("clips", "frames"), None, None, "heads"),
        P("clips", "frames", "heads"),
        P("clips", None, "heads"),
    )
    return jax.shard_map(shards, mesh=mesh, in_specs=in_specs, out_specs=out_specs, check_vma=False)
```

```python
import functools
import math

import jax
import jax.numpy as jnp
from jax import lax
from jax.experimental import pallas as pl
from jax.experimental.pallas import tpu as pltpu
from jax.sharding import PartitionSpec as P

HEADS = 8
LANES = 128
F32 = jnp.float32
BF16 = jnp.bfloat16
PARAMS = pltpu.CompilerParams(vmem_limit_bytes=56 * 1024 * 1024)
NN = (((1,), (0,)), ((), ()))
NT = (((1,), (1,)), ((), ()))
TN = (((0,), (0,)), ((), ()))


def mul(left, right, dims=NN):
    return lax.dot_general(left, right, dims, preferred_element_type=F32)


def vmem():
    return pl.BlockSpec(memory_space=pltpu.VMEM)


def smem():
    return pl.BlockSpec(memory_space=pltpu.SMEM)


def lane_tiles(channels):
    return [
        (k, k * LANES, min(LANES, channels - k * LANES)) for k in range(pl.cdiv(channels, LANES))
    ]


def pool_body(geometry, place, own, other, weights, taps, to_pair, to_next, middle, windows, wide):
    rows, cols, local = geometry
    pooled_rows, pooled_cols = rows // 4, cols // 4
    even = place[0] % 2 == 0
    starts = lax.broadcasted_iota(jnp.int32, (pooled_cols, LANES), 0) == 0
    for side in range(2):
        full = mul(own[...], weights[side + 1, :local, :]) + mul(
            other[...], weights[side + 1, local:, :]
        )
        full = full.astype(BF16).astype(F32)
        for tile, low, width in lane_tiles(local):
            wide[tile, 0:8, :] = jnp.zeros((8, LANES), F32)
            wide[tile, 8:, :width] = full[:, low : low + width]
            for b in range(3):
                for e in range(3):
                    for i in range(pooled_rows):
                        row = 4 * i + b - 1
                        if row < 0:
                            piece = jnp.zeros((pooled_cols, LANES), F32)
                        else:
                            piece = wide[tile, pl.ds(row * cols + e + 7, pooled_cols, stride=4), :]
                            if e == 0:
                                piece = jnp.where(starts, 0.0, piece)
                        at = slice(i * pooled_cols, (i + 1) * pooled_cols)
                        windows[side, 3 * b + e, at, low : low + width] = piece[:, :width]
        sums = []
        for a in range(3):
            total = windows[side, 0] * taps[side, 9 * a : 9 * a + 1, :]
            for k in range(1, 9):
                total = total + windows[side, k] * taps[side, 9 * a + k : 9 * a + k + 1, :]
            sums.append(total)
        lanes = slice(side * local, (side + 1) * local)
        earlier, center, later = sums
        to_pair[:, lanes] = jnp.where(even, earlier, later).astype(BF16)
        to_next[:, lanes] = jnp.where(even, later, earlier).astype(BF16)
        middle[:, lanes] = center


def pool_call(place, own, other, weights, taps, rows, cols):
    local = own.shape[1]
    count = rows * cols // 16
    return pl.pallas_call(
        functools.partial(pool_body, (rows, cols, local)),
        out_shape=(
            jax.ShapeDtypeStruct((count, 2 * local), BF16),
            jax.ShapeDtypeStruct((count, 2 * local), BF16),
            jax.ShapeDtypeStruct((count, 2 * local), F32),
            jax.ShapeDtypeStruct((2, 9, count, local), F32),
        ),
        in_specs=[smem()] + [vmem()] * 4,
        out_specs=(vmem(),) * 4,
        scratch_shapes=[pltpu.VMEM((pl.cdiv(local, LANES), rows * cols + 8, LANES), F32)],
        compiler_params=PARAMS,
        name="project_pool",
    )(place, own, other, weights, taps)


def spread_rows(head_dim, local, heads):
    rows = lax.broadcasted_iota(jnp.int32, (heads * LANES, local), 0)
    cols = lax.broadcasted_iota(jnp.int32, (heads * LANES, local), 1)
    chosen = rows < 0
    for h in range(heads):
        inside = (cols >= h * head_dim) & (cols < (h + 1) * head_dim)
        chosen = chosen | (inside & (rows == cols + h * (LANES - head_dim)))
    return chosen.astype(F32).astype(BF16)


def query_body(geometry, own, other, near_t, far_t, out_grad, query_t, grad_t):
    head_dim, local, heads = geometry
    spread = spread_rows(head_dim, local, heads)
    near = mul(spread, near_t[...]).astype(BF16)
    far = mul(spread, far_t[...]).astype(BF16)
    query = mul(near, own[...], NT) + mul(far, other[...], NT)
    query_t[...] = query.astype(BF16)
    grad_t[...] = mul(spread, out_grad[...], NT).astype(BF16)


def query_call(own, other, near, far, out_grad, head_dim):
    tokens, local = own.shape
    heads = local // head_dim
    shape = jax.ShapeDtypeStruct((heads * LANES, tokens), BF16)
    return pl.pallas_call(
        functools.partial(query_body, (head_dim, local, heads)),
        out_shape=(shape, shape),
        in_specs=[vmem()] * 5,
        out_specs=(vmem(),) * 2,
        compiler_params=PARAMS,
        name="project_query",
    )(own, other, near, far, out_grad)


def attend_body(geometry, keys, query_t, grad_t, key_grads, query_grad, total):
    head_dim, local, heads = geometry
    head = pl.program_id(0)
    scale = head_dim ** (-0.5)
    rows = lax.broadcasted_iota(jnp.int32, (2 * local, 2 * LANES), 0)
    cols = lax.broadcasted_iota(jnp.int32, (2 * local, 2 * LANES), 1)
    lane = cols % LANES
    source = lane + (cols // LANES) * local + head * head_dim
    chosen = ((rows == source) & (lane < head_dim)).astype(F32).astype(BF16)
    both = mul(keys[...], chosen).astype(BF16)
    key, value = both[:, :LANES], both[:, LANES:]
    query = query_t[...]
    grad = grad_t[...]
    scores = mul(key, query)
    raised = jnp.exp2(scores * (scale * math.log2(math.e)))
    inverse = 1.0 / jnp.sum(raised, axis=0, keepdims=True)
    prob_grad = mul(value, grad)
    centre = jnp.sum(raised * prob_grad, axis=0, keepdims=True) * inverse
    probs = raised * inverse
    score_grad = (probs * (prob_grad - centre) * scale).astype(BF16)
    value_back = mul(probs.astype(BF16), grad, NT)
    key_back = mul(score_grad, query, NT)
    square = lax.broadcasted_iota(jnp.int32, (LANES, LANES), 0) == lax.broadcasted_iota(
        jnp.int32, (LANES, LANES), 1
    )
    key_t = mul(square.astype(F32).astype(BF16), key, NT).astype(BF16)
    back_t = mul(key_t, score_grad) + grad.astype(F32)
    query_grad[...] = back_t.T.astype(BF16)
    joined = jnp.concatenate([key_back, value_back], axis=1).astype(BF16)
    placed = mul(joined, chosen, NT)

    @pl.when(head == 0)
    def _():
        total[...] = placed

    @pl.when(head > 0)
    def _():
        total[...] += placed

    @pl.when(head == heads - 1)
    def _():
        key_grads[...] = total[...].astype(BF16)


def attend_call(keys, query_t, grad_t, head_dim):
    key_count, both = keys.shape
    local = both // 2
    heads = local // head_dim
    tokens = query_t.shape[1]
    return pl.pallas_call(
        functools.partial(attend_body, (head_dim, local, heads)),
        grid=(heads,),
        out_shape=(
            jax.ShapeDtypeStruct((key_count, both), BF16),
            jax.ShapeDtypeStruct((tokens, heads * LANES), BF16),
        ),
        in_specs=[
            pl.BlockSpec((key_count, both), lambda h: (0, 0)),
            pl.BlockSpec((LANES, tokens), lambda h: (h, 0)),
            pl.BlockSpec((LANES, tokens), lambda h: (h, 0)),
        ],
        out_specs=(
            pl.BlockSpec((key_count, both), lambda h: (0, 0)),
            pl.BlockSpec((tokens, LANES), lambda h: (0, h)),
        ),
        scratch_shapes=[pltpu.VMEM((key_count, both), F32)],
        compiler_params=PARAMS,
        name="attend_backward",
    )(keys, query_t, grad_t)


def query_side_body(geometry, query_pad, own, other, weights, weight_terms, token_terms):
    head_dim, local, heads = geometry
    spread = spread_rows(head_dim, local, heads)
    query_back = mul(query_pad[...], spread).astype(BF16)
    weight_terms[:local, :] = mul(own[...], query_back, TN)
    weight_terms[local:, :] = mul(other[...], query_back, TN)
    token_terms[0] = mul(query_back, weights[0, :local, :], NT)
    token_terms[1] = mul(query_back, weights[0, local:, :], NT)


def query_side_call(query_pad, own, other, weights, head_dim):
    tokens, local = own.shape
    return pl.pallas_call(
        functools.partial(query_side_body, (head_dim, local, local // head_dim)),
        out_shape=(
            jax.ShapeDtypeStruct((2 * local, local), F32),
            jax.ShapeDtypeStruct((2, tokens, local), F32),
        ),
        in_specs=[vmem()] * 4,
        out_specs=(vmem(),) * 2,
        compiler_params=PARAMS,
        name="query_side",
    )(query_pad, own, other, weights)


def pull_body(
    geometry,
    place,
    mine,
    before,
    after,
    windows,
    taps,
    own,
    other,
    weights,
    query_weight,
    query_token,
    here,
    away,
    token_near,
    token_far,
    wide,
    staged,
    folded,
):
    rows, cols, local, count = geometry
    pooled_rows, pooled_cols = rows // 4, cols // 4
    position, core = place[0], place[1]
    pooled = pooled_rows * pooled_cols
    block_rows = 2 * local // count
    outer = count // 2
    starts = lax.broadcasted_iota(jnp.int32, (pooled, local), 0) % pooled_cols == 0
    here[outer * block_rows :, :] = jnp.zeros((here.shape[0] - outer * block_rows, 3 * local), F32)
    away[outer * block_rows :, :] = jnp.zeros((here.shape[0] - outer * block_rows, 3 * local), BF16)
    near = query_token[0]
    far = query_token[1]
    columns = [(query_weight[:local, :], query_weight[local:, :])]
    for side in range(2):
        lanes = slice(side * local, (side + 1) * local)
        grads = [after[:, lanes].astype(F32), mine[:, lanes], before[:, lanes].astype(F32)]
        wide[...] = jnp.zeros(wide.shape, F32)
        for b in range(3):
            for e in range(3):
                k = 3 * b + e
                window = windows[side, k]
                spread = None
                for a in range(3):
                    term = grads[a] * taps[side, 9 * a + k : 9 * a + k + 1, :]
                    spread = term if spread is None else spread + term
                    tap = jnp.sum(grads[a] * window, axis=0, keepdims=True)
                    at = outer * block_rows + 9 * a + k
                    here[at : at + 1, lanes] = tap
                    folded[9 * a + k : 9 * a + k + 1, lanes] = tap
                if e == 0:
                    spread = jnp.where(starts, 0.0, spread)
                for tile, low, width in lane_tiles(local):
                    part = spread[:, low : low + width]
                    if width < LANES:
                        part = jnp.concatenate(
                            [part, jnp.zeros((pooled, LANES - width), F32)], axis=1
                        )
                    staged[tile] = part
                    for i in range(pooled_rows):
                        row = 4 * i + b - 1
                        if row >= 0:
                            at = slice(i * pooled_cols, (i + 1) * pooled_cols)
                            wide[tile, pl.ds(row * cols + e + 7, pooled_cols, stride=4), :] = (
                                staged[tile, at, :]
                            )
        back = jnp.concatenate(
            [wide[tile, 8:, :width] for tile, low, width in lane_tiles(local)], axis=1
        ).astype(BF16)
        near = near + mul(back, weights[side + 1, :local, :], NT)
        far = far + mul(back, weights[side + 1, local:, :], NT)
        columns.append((mul(own[...], back, TN), mul(other[...], back, TN)))
    token_near[...] = near
    token_far[...] = far.astype(BF16)
    away[outer * block_rows : outer * block_rows + 32, : 2 * local] = folded[...].astype(BF16)
    for half in range(2):
        actual = jnp.where(half == 0, core, 1 - core)
        for j in range(count // 2):
            relative = position ^ (actual * (count // 2) + j)
            at = pl.multiple_of((relative // 2) * block_rows, 8)
            rows_here = slice(j * block_rows, (j + 1) * block_rows)
            for side in range(3):
                lanes = slice(side * local, (side + 1) * local)
                value = columns[side][half][rows_here, :]

                @pl.when(relative % 2 == 0)
                def _(value=value, at=at, lanes=lanes):
                    here[pl.ds(at, block_rows), lanes] = value

                @pl.when(relative % 2 == 1)
                def _(value=value, at=at, lanes=lanes):
                    away[pl.ds(at, block_rows), lanes] = value.astype(BF16)


def pull_call(place, mine, before, after, windows, taps, own, other, weights, query_weight, query_token, rows, cols, count):
    tokens, local = own.shape
    half = local
    size = half + 32
    return pl.pallas_call(
        functools.partial(pull_body, (rows, cols, local, count)),
        out_shape=(
            jax.ShapeDtypeStruct((size, 3 * local), F32),
            jax.ShapeDtypeStruct((size, 3 * local), BF16),
            jax.ShapeDtypeStruct((tokens, local), F32),
            jax.ShapeDtypeStruct((tokens, local), BF16),
        ),
        in_specs=[smem()] + [vmem()] * 10,
        out_specs=(vmem(),) * 4,
        scratch_shapes=[
            pltpu.VMEM((pl.cdiv(local, LANES), tokens + 8, LANES), F32),
            pltpu.VMEM((pl.cdiv(local, LANES), rows * cols // 16, LANES), F32),
            pltpu.VMEM((32, 2 * local), F32),
        ],
        compiler_params=PARAMS,
        name="pull_back",
    )(place, mine, before, after, windows, taps, own, other, weights, query_weight, query_token)


def frame_pairs(step, flip):
    count = lax.axis_size("frames")
    return [(i, i ^ (2 * step + flip)) for i in range(count)]


def next_pairs():
    count = lax.axis_size("frames")
    return [(i, (i + (1 if i % 2 else -1)) % count) for i in range(count)]


def exchange(block, pairs):
    return lax.ppermute(block, "frames", pairs)


def gather_frames(block):
    outer = lax.axis_size("frames") // 2
    same = [block] + [exchange(block, frame_pairs(s, 0)) for s in range(1, outer)]
    other = exchange(jnp.concatenate(same), frame_pairs(0, 1))
    return jnp.concatenate(same + [other])


def scatter_frames(terms):
    outer = lax.axis_size("frames") // 2
    half = terms.shape[0] // 2
    moved = exchange(terms[half:], frame_pairs(0, 1))
    summed = terms[:half].astype(F32) + moved.astype(F32)
    rows = half // outer
    low = summed.astype(BF16)
    own = summed[:rows]
    for step in range(1, outer):
        piece = low[step * rows : (step + 1) * rows]
        own = own + exchange(piece, frame_pairs(step, 0)).astype(F32)
    return own


def scatter_weights(here, away, rows):
    outer = lax.axis_size("frames") // 2
    moved = exchange(away, frame_pairs(0, 1))
    summed = here + moved.astype(F32)
    tail = summed[outer * rows :]
    own = jnp.concatenate([summed[:rows], tail])
    low = summed.astype(BF16)
    for step in range(1, outer):
        piece = jnp.concatenate([low[step * rows : (step + 1) * rows], low[outer * rows :]])
        own = own + exchange(piece, frame_pairs(step, 0)).astype(F32)
    return own[:rows], own[rows:]


def shards(tokens, out_grad, w_qkv, pool_kernel):
    local = tokens.shape[-1]
    heads_here = HEADS // lax.axis_size("heads")
    head_dim = local // heads_here
    rows, cols = tokens.shape[1], tokens.shape[2]
    token_count = rows * cols
    count = lax.axis_size("frames")
    frame = lax.axis_index("frames")
    core = lax.axis_index("heads")
    even = frame % 2 == 0
    place = jnp.stack([frame, core]).astype(jnp.int32)
    own = tokens.reshape(token_count, local)
    grad = out_grad.reshape(token_count, local)
    other = lax.ppermute(own, "heads", [(0, 1), (1, 0)])
    weights = jnp.where(core == 0, w_qkv, jnp.roll(w_qkv, local, axis=1))
    to_pair, to_next, middle, windows = pool_call(
        place, own, other, weights, pool_kernel, rows, cols
    )
    from_pair = exchange(to_pair, frame_pairs(0, 1))
    from_next = exchange(to_next, next_pairs())
    at_end = (frame == 0) | (frame == count - 1)
    pooled = middle + from_pair.astype(F32) + jnp.where(at_end, 0.0, from_next.astype(F32))
    query_t, grad_t = query_call(
        own, other, weights[0, :local].T, weights[0, local:].T, grad, head_dim
    )
    keys = gather_frames(pooled.astype(BF16))
    key_grads, query_pad = attend_call(keys, query_t, grad_t, head_dim)
    owned = scatter_frames(key_grads)
    query_weight, query_token = query_side_call(query_pad, own, other, weights, head_dim)
    low = owned.astype(BF16)
    pair = exchange(low, frame_pairs(0, 1))
    beside = jnp.where(at_end, 0.0, exchange(low, next_pairs()).astype(F32)).astype(BF16)
    before = jnp.where(even, beside, pair)
    after = jnp.where(even, pair, beside)
    here, away, near, far = pull_call(
        place, owned, before, after, windows, pool_kernel, own, other, weights,
        query_weight, query_token, rows, cols, count,
    )
    weight_part, kernel_part = scatter_weights(here, away, 2 * local // count)
    weight_grad = jnp.stack([weight_part[:, s * local : (s + 1) * local] for s in range(3)])
    kernel_grad = jnp.stack([kernel_part[:27, s * local : (s + 1) * local] for s in range(2)])
    input_grad = near + lax.ppermute(far, "heads", [(0, 1), (1, 0)]).astype(F32)
    return input_grad.astype(BF16).reshape(tokens.shape), weight_grad, kernel_grad


def solution(mesh):
    in_specs = (
        P(("clips", "frames"), None, None, "heads"),
        P(("clips", "frames"), None, None, "heads"),
        P(None, None, "heads"),
        P(None, None, "heads"),
    )
    out_specs = (
        P(("clips", "frames"), None, None, "heads"),
        P("clips", "frames", "heads"),
        P("clips", None, "heads"),
    )
    return jax.shard_map(shards, mesh=mesh, in_specs=in_specs, out_specs=out_specs, check_vma=False)
```

```python
import functools
import math

import jax
import jax.numpy as jnp
from jax import lax
from jax.experimental import pallas as pl
from jax.experimental.pallas import tpu as pltpu
from jax.sharding import PartitionSpec as P

HEADS = 8
LANES = 128
F32 = jnp.float32
BF16 = jnp.bfloat16
PARAMS = pltpu.CompilerParams(vmem_limit_bytes=16 * 1024 * 1024)
NN = (((1,), (0,)), ((), ()))
NT = (((1,), (1,)), ((), ()))
TN = (((0,), (0,)), ((), ()))


def mul(left, right, dims=NN):
    return lax.dot_general(left, right, dims, preferred_element_type=F32)


def near_core(*arrays):
    return tuple(pltpu.with_memory_space_constraint(x, pltpu.VMEM) for x in arrays)


def vmem():
    return pl.BlockSpec(memory_space=pltpu.VMEM)


def smem():
    return pl.BlockSpec(memory_space=pltpu.SMEM)


def lane_tiles(channels):
    return [
        (k, k * LANES, min(LANES, channels - k * LANES)) for k in range(pl.cdiv(channels, LANES))
    ]


def round_up(size, step):
    return pl.cdiv(size, step) * step


def pool_body(
    geometry, place, own, other, weights, taps, to_pair, to_next, inner, stored, windows, wide
):
    rows, cols, local = geometry
    pooled_rows, pooled_cols = rows // 4, cols // 4
    even = place[0] % 2 == 0
    first = place[1] == 0
    mine, theirs = own[:, :local].astype(F32), other[:, :local].astype(F32)
    low_half = jnp.where(first, mine, theirs)
    high_half = jnp.where(first, theirs, mine)
    joined = jnp.concatenate([low_half, high_half], axis=1).astype(BF16)
    starts = lax.broadcasted_iota(jnp.int32, (pooled_cols, LANES), 0) == 0
    for side in range(2):
        full = mul(joined, weights[side + 1], NT).astype(BF16).astype(F32)
        for tile, low, width in lane_tiles(local):
            wide[tile, 0:8, :] = jnp.zeros((8, LANES), F32)
            wide[tile, 8:, :width] = full[:, low : low + width]
            for b in range(3):
                for e in range(3):
                    for i in range(pooled_rows):
                        row = 4 * i + b - 1
                        if row < 0:
                            piece = jnp.zeros((pooled_cols, LANES), F32)
                        else:
                            piece = wide[tile, pl.ds(row * cols + e + 7, pooled_cols, stride=4), :]
                            if e == 0:
                                piece = jnp.where(starts, 0.0, piece)
                        at = slice(i * pooled_cols, (i + 1) * pooled_cols)
                        windows[3 * b + e, at, low : low + width] = piece[:, :width]
        for k in range(9):
            stored[side, k] = windows[k].astype(BF16)
        sums = []
        for a in range(3):
            total = windows[0] * taps[9 * a, side : side + 1, :]
            for k in range(1, 9):
                total = total + windows[k] * taps[9 * a + k, side : side + 1, :]
            sums.append(total)
        lanes = slice(side * local, (side + 1) * local)
        earlier, center, later = sums
        to_pair[:, lanes] = center.astype(BF16)
        to_next[:, lanes] = jnp.where(even, later, earlier).astype(BF16)
        inner[:, lanes] = jnp.where(even, earlier, later)


def pool_call(place, own, other, weights, taps, rows, cols):
    local = weights.shape[1]
    count = rows * cols // 16
    return pl.pallas_call(
        functools.partial(pool_body, (rows, cols, local)),
        out_shape=(
            pltpu.VMEM((count, 2 * local), BF16),
            pltpu.VMEM((count, 2 * local), BF16),
            pltpu.VMEM((count, 2 * local), F32),
            jax.ShapeDtypeStruct((2, 9, count, local), BF16),
        ),
        in_specs=[smem()] + [vmem()] * 4,
        out_specs=(vmem(),) * 4,
        scratch_shapes=[
            pltpu.VMEM((9, count, local), F32),
            pltpu.VMEM((pl.cdiv(local, LANES), rows * cols + 8, LANES), F32)],
        compiler_params=PARAMS,
        name="project_pool",
    )(place, *near_core(own, other), weights, taps)


def spread_rows(head_dim, local, heads):
    rows = lax.broadcasted_iota(jnp.int32, (heads * LANES, local), 0)
    cols = lax.broadcasted_iota(jnp.int32, (heads * LANES, local), 1)
    chosen = rows < 0
    for h in range(heads):
        inside = (cols >= h * head_dim) & (cols < (h + 1) * head_dim)
        chosen = chosen | (inside & (rows == cols + h * (LANES - head_dim)))
    return chosen.astype(F32).astype(BF16)


def identity(size):
    rows = lax.broadcasted_iota(jnp.int32, (size, size), 0)
    cols = lax.broadcasted_iota(jnp.int32, (size, size), 1)
    return (rows == cols).astype(F32).astype(BF16)


def query_body(geometry, place, own, other, weights, out_grad, query_t, grad_t, tokens_t):
    head_dim, local, heads = geometry
    spread = spread_rows(head_dim, local, heads)
    turn = identity(local)
    near = pl.multiple_of(place[1] * local, 16)
    far = pl.multiple_of((1 - place[1]) * local, 16)
    tokens_t[pl.ds(near, local), :] = mul(turn, own[:, :local], NT).astype(BF16)
    tokens_t[pl.ds(far, local), :] = mul(turn, other[:, :local], NT).astype(BF16)
    query_t[...] = mul(mul(spread, weights[0]).astype(BF16), tokens_t[...]).astype(BF16)
    grad_t[...] = mul(spread, out_grad[...], NT).astype(BF16)


def query_call(place, own, other, weights, out_grad, head_dim):
    tokens, local = out_grad.shape
    heads = local // head_dim
    shape = pltpu.VMEM((heads * LANES, tokens), BF16)
    return pl.pallas_call(
        functools.partial(query_body, (head_dim, local, heads)),
        out_shape=(shape, shape, pltpu.VMEM((2 * local, tokens), BF16)),
        in_specs=[smem()] + [vmem()] * 4,
        out_specs=(vmem(),) * 3,
        compiler_params=PARAMS,
        name="project_query",
    )(place, *near_core(own, other), weights, out_grad)


def choose_head(head_dim, local, head):
    rows = lax.broadcasted_iota(jnp.int32, (2 * local, 2 * LANES), 0)
    cols = lax.broadcasted_iota(jnp.int32, (2 * local, 2 * LANES), 1)
    lane = cols % LANES
    source = lane + (cols // LANES) * local + head * head_dim
    return ((rows == source) & (lane < head_dim)).astype(F32).astype(BF16)


def head_products(head_dim, keys, chosen, query, grad):
    both = mul(keys, chosen).astype(BF16)
    key, value = both[:, :LANES], both[:, LANES:]
    factor = head_dim ** (-0.5) * math.log2(math.e)
    raised = jnp.exp2(mul(key, query) * factor)
    return key, raised, mul(value, grad)


def measure_body(geometry, keys, query_t, grad_t, sums):
    head_dim, local, heads = geometry
    chosen = choose_head(head_dim, local, pl.program_id(0))
    key, raised, prob_grad = head_products(head_dim, keys[...], chosen, query_t[...], grad_t[...])
    sums[0, 0:1, :] = jnp.sum(raised, axis=0, keepdims=True)
    sums[0, 1:2, :] = jnp.sum(raised * prob_grad, axis=0, keepdims=True)


def attend_body(geometry, final, keys, query_t, grad_t, sums, *rest):
    head_dim, local, heads = geometry
    if final:
        partial_t, key_grads, query_grad, total = rest
    else:
        key_grads, totals, partial_t, total = rest
    head = pl.program_id(0)
    scale = head_dim ** (-0.5)
    chosen = choose_head(head_dim, local, head)
    query, grad = query_t[...], grad_t[...]
    key, raised, prob_grad = head_products(head_dim, keys[...], chosen, query, grad)
    if final:
        inverse, centre = sums[0, 0:1, :], sums[0, 1:2, :]
    else:
        inverse = 1.0 / (sums[0, 0:1, :] + jnp.sum(raised, axis=0, keepdims=True))
        weighted = sums[0, 1:2, :] + jnp.sum(raised * prob_grad, axis=0, keepdims=True)
        centre = weighted * inverse
        totals[0, 0:1, :] = inverse
        totals[0, 1:2, :] = centre
    probs = raised * inverse
    score_grad = (probs * (prob_grad - centre) * scale).astype(BF16)
    value_back = mul(probs.astype(BF16), grad, NT)
    key_back = mul(score_grad, query, NT)
    key_t = mul(identity(LANES), key, NT).astype(BF16)
    back_t = mul(key_t, score_grad)
    if final:
        query_grad[...] = (back_t + partial_t[...] + grad.astype(F32)).T.astype(BF16)
    else:
        partial_t[...] = back_t
    joined = jnp.concatenate([key_back, value_back], axis=1).astype(BF16)
    placed = mul(joined, chosen, NT)

    @pl.when(head == 0)
    def _():
        total[...] = placed

    @pl.when(head > 0)
    def _():
        total[...] += placed

    @pl.when(head == heads - 1)
    def _():
        key_grads[...] = total[...].astype(BF16)


def attend_specs(keys, query_t):
    key_count, both = keys.shape
    tokens = query_t.shape[1]
    key_spec = pl.BlockSpec((key_count, both), lambda h: (0, 0))
    lane_spec = pl.BlockSpec((LANES, tokens), lambda h: (h, 0))
    sum_spec = pl.BlockSpec((1, 8, tokens), lambda h: (h, 0, 0))
    return key_spec, lane_spec, sum_spec


def measure_call(keys, query_t, grad_t, head_dim):
    local, tokens = keys.shape[1] // 2, query_t.shape[1]
    heads = local // head_dim
    key_spec, lane_spec, sum_spec = attend_specs(keys, query_t)
    return pl.pallas_call(
        functools.partial(measure_body, (head_dim, local, heads)),
        grid=(heads,),
        out_shape=pltpu.VMEM((heads, 8, tokens), F32),
        in_specs=[key_spec, lane_spec, lane_spec],
        out_specs=sum_spec,
        compiler_params=PARAMS,
        name="attend_measure",
    )(*near_core(keys, query_t, grad_t))


def attend_call(keys, query_t, grad_t, sums, head_dim):
    key_count, both = keys.shape
    local, tokens = both // 2, query_t.shape[1]
    heads = local // head_dim
    key_spec, lane_spec, sum_spec = attend_specs(keys, query_t)
    return pl.pallas_call(
        functools.partial(attend_body, (head_dim, local, heads), False),
        grid=(heads,),
        out_shape=(
            pltpu.VMEM((key_count, both), BF16),
            pltpu.VMEM((heads, 8, tokens), F32),
            pltpu.VMEM((heads * LANES, tokens), F32),
        ),
        in_specs=[key_spec, lane_spec, lane_spec, sum_spec],
        out_specs=(key_spec, sum_spec, lane_spec),
        scratch_shapes=[pltpu.VMEM((key_count, both), F32)],
        compiler_params=PARAMS,
        name="attend_other",
    )(*near_core(keys, query_t, grad_t, sums))


def attend_final_call(keys, query_t, grad_t, totals, partial_t, head_dim):
    key_count, both = keys.shape
    local, tokens = both // 2, query_t.shape[1]
    heads = local // head_dim
    key_spec, lane_spec, sum_spec = attend_specs(keys, query_t)
    return pl.pallas_call(
        functools.partial(attend_body, (head_dim, local, heads), True),
        grid=(heads,),
        out_shape=(
            pltpu.VMEM((key_count, both), BF16),
            pltpu.VMEM((tokens, heads * LANES), BF16),
        ),
        in_specs=[key_spec, lane_spec, lane_spec, sum_spec, lane_spec],
        out_specs=(key_spec, pl.BlockSpec((tokens, LANES), lambda h: (0, h))),
        scratch_shapes=[pltpu.VMEM((key_count, both), F32)],
        compiler_params=PARAMS,
        name="attend_same",
    )(*near_core(keys, query_t, grad_t, totals, partial_t))


def store_blocks(position, count, rows, columns, here, away):
    padded = round_up(rows, 8)
    for j in range(count):
        relative = position ^ j
        at = pl.multiple_of((relative // 2) * padded, 8)
        block = slice(j * rows, (j + 1) * rows)
        value = jnp.concatenate([column[block, :] for column in columns], axis=1)

        @pl.when(relative % 2 == 0)
        def _(value=value, at=at):
            here[pl.ds(at, rows), : value.shape[1]] = value

        @pl.when(relative % 2 == 1)
        def _(value=value, at=at):
            away[pl.ds(at, rows), : value.shape[1]] = value.astype(BF16)


def query_side_body(geometry, place, query_pad, tokens_t, query_back, here, away):
    head_dim, local, heads, count = geometry
    spread = spread_rows(head_dim, local, heads)
    back = mul(query_pad[...], spread).astype(BF16)
    query_back[...] = back
    here[...] = jnp.zeros(here.shape, F32)
    away[...] = jnp.zeros(away.shape, BF16)
    column = mul(tokens_t[...], back)
    store_blocks(place[0], count, 2 * local // count, [column], here, away)


def query_side_call(place, query_pad, tokens_t, head_dim, count):
    both, tokens = tokens_t.shape
    local = both // 2
    shape = (count // 2 * round_up(both // count, 8), round_up(local, LANES))
    return pl.pallas_call(
        functools.partial(query_side_body, (head_dim, local, local // head_dim, count)),
        out_shape=(
            pltpu.VMEM((tokens, local), BF16),
            pltpu.VMEM(shape, F32),
            pltpu.VMEM(shape, BF16),
        ),
        in_specs=[smem()] + [vmem()] * 2,
        out_specs=(vmem(),) * 3,
        compiler_params=PARAMS,
        name="query_side",
    )(place, *near_core(query_pad, tokens_t))


def pull_body(
    geometry,
    place,
    mine,
    swapped,
    beside,
    windows,
    taps,
    tokens_t,
    weights,
    query_back,
    here,
    away,
    token_near,
    token_far,
    wide,
    staged,
    folded,
):
    rows, cols, local, count = geometry
    pooled_rows, pooled_cols = rows // 4, cols // 4
    position, core = place[0], place[1]
    even = position % 2 == 0
    pooled = pooled_rows * pooled_cols
    block_rows = 2 * local // count
    outer = count // 2
    starts = lax.broadcasted_iota(jnp.int32, (pooled, local), 0) % pooled_cols == 0
    folded[...] = jnp.zeros(folded.shape, F32)
    here[...] = jnp.zeros(here.shape, F32)
    away[...] = jnp.zeros(away.shape, BF16)
    token_sum = mul(query_back[...], weights[0])
    columns = []
    for side in range(2):
        lanes = slice(side * local, (side + 1) * local)
        partner, distant = swapped[:, lanes].astype(F32), beside[:, lanes].astype(F32)
        grads = [
            jnp.where(even, partner, distant),
            mine[:, lanes].astype(F32),
            jnp.where(even, distant, partner),
        ]
        wide[...] = jnp.zeros(wide.shape, F32)
        for b in range(3):
            for e in range(3):
                k = 3 * b + e
                window = windows[side, k].astype(F32)
                spread = None
                for a in range(3):
                    term = grads[a] * taps[9 * a + k, side : side + 1, :]
                    spread = term if spread is None else spread + term
                    tap = jnp.sum(grads[a] * window, axis=0, keepdims=True)
                    folded[9 * a + k : 9 * a + k + 1, lanes] = tap
                if e == 0:
                    spread = jnp.where(starts, 0.0, spread)
                for tile, low, width in lane_tiles(local):
                    part = spread[:, low : low + width]
                    if width < LANES:
                        part = jnp.concatenate(
                            [part, jnp.zeros((pooled, LANES - width), F32)], axis=1
                        )
                    staged[tile] = part
                    for i in range(pooled_rows):
                        row = 4 * i + b - 1
                        if row >= 0:
                            at = slice(i * pooled_cols, (i + 1) * pooled_cols)
                            wide[tile, pl.ds(row * cols + e + 7, pooled_cols, stride=4), :] = (
                                staged[tile, at, :]
                            )
        back = jnp.concatenate(
            [wide[tile, 8:, :width] for tile, low, width in lane_tiles(local)], axis=1
        ).astype(BF16)
        token_sum = token_sum + mul(back, weights[side + 1])
        columns.append(mul(tokens_t[...], back))
    first = core == 0
    low_half, high_half = token_sum[:, :local], token_sum[:, local:]
    token_near[...] = jnp.where(first, low_half, high_half)
    token_far[:, :local] = jnp.where(first, high_half, low_half).astype(BF16)
    token_far[:, local:] = jnp.zeros((token_far.shape[0], token_far.shape[1] - local), BF16)
    blocks_end = outer * round_up(block_rows, 8)
    here[blocks_end:, :] = folded[...]
    away[blocks_end:, :] = folded[...].astype(BF16)
    store_blocks(position, count, block_rows, columns, here, away)


def pull_call(
    place, mine, swapped, beside, windows, taps, tokens_t, weights, query_back, rows, cols, count
):
    both, tokens = tokens_t.shape
    local = both // 2
    size = count // 2 * round_up(both // count, 8) + 32
    tiles = pl.cdiv(local, LANES)
    return pl.pallas_call(
        functools.partial(pull_body, (rows, cols, local, count)),
        out_shape=(
            pltpu.VMEM((size, both), F32),
            pltpu.VMEM((size, both), BF16),
            pltpu.VMEM((tokens, local), F32),
            pltpu.VMEM((tokens, tiles * LANES), BF16),
        ),
        in_specs=[smem()] + [vmem()] * 8,
        out_specs=(vmem(),) * 4,
        scratch_shapes=[
            pltpu.VMEM((tiles, tokens + 8, LANES), F32),
            pltpu.VMEM((tiles, rows * cols // 16, LANES), F32),
            pltpu.VMEM((32, both), F32),
        ],
        compiler_params=PARAMS,
        name="pull_back",
    )(
        place,
        *near_core(mine, swapped, beside),
        windows,
        taps,
        *near_core(tokens_t),
        weights,
        *near_core(query_back),
    )


def frame_pairs(step, flip):
    count = lax.axis_size("frames")
    return [(i, i ^ (2 * step + flip)) for i in range(count)]


def outer_pairs(direction):
    count = lax.axis_size("frames")
    moves = [(i, i + direction * (2 if i % 2 else -2)) for i in range(count)]
    return [(i, j) for i, j in moves if 0 <= j < count]


def exchange(block, pairs):
    return lax.ppermute(block, "frames", pairs)


def across(block):
    return lax.ppermute(block, "heads", [(0, 1), (1, 0)])


def scatter_weights(here, moved, rows):
    outer = lax.axis_size("frames") // 2
    summed = here + moved.astype(F32)
    end = outer * rows
    own = jnp.concatenate([summed[:rows], summed[end:]])
    low = summed.astype(BF16)
    pieces = []
    for step in range(1, outer):
        piece = jnp.concatenate([low[step * rows : (step + 1) * rows], low[end:]])
        pieces.append(exchange(piece, frame_pairs(step, 0)))
    return own, pieces


def add_all(own, pieces):
    for piece in pieces:
        own = own + piece.astype(F32)
    return own


def shards(tokens, out_grad, w_qkv, pool_kernel):
    local = tokens.shape[-1]
    heads_here = HEADS // lax.axis_size("heads")
    head_dim = local // heads_here
    rows, cols = tokens.shape[1], tokens.shape[2]
    token_count = rows * cols
    count = lax.axis_size("frames")
    frame = lax.axis_index("frames")
    core = lax.axis_index("heads")
    place = jnp.stack([frame, core]).astype(jnp.int32)
    outer = count // 2
    spare = round_up(local, LANES) - local
    own = jnp.pad(tokens.reshape(token_count, local), ((0, 0), (0, spare)))
    grad = out_grad.reshape(token_count, local)
    other = across(own)
    weights = w_qkv.transpose(0, 2, 1)
    taps = pool_kernel.transpose(1, 0, 2)
    to_pair, to_next, inner, windows = pool_call(place, own, other, weights, taps, rows, cols)
    from_next = exchange(to_next, outer_pairs(1))
    from_pair = exchange(to_pair, frame_pairs(0, 1))
    block = (inner + from_pair.astype(F32) + from_next.astype(F32)).astype(BF16)
    others = [exchange(block, frame_pairs(s, 0)) for s in range(1, outer)]
    query_t, grad_t, tokens_t = query_call(place, own, other, weights, grad, head_dim)
    others, query_t, grad_t, tokens_t = lax.optimization_barrier(
        (others, query_t, grad_t, tokens_t)
    )
    same_keys = jnp.concatenate([block] + others)
    other_keys = exchange(same_keys, frame_pairs(0, 1))
    sums = measure_call(same_keys, query_t, grad_t, head_dim)
    other_grads, totals, partial_t = attend_call(other_keys, query_t, grad_t, sums, head_dim)
    moved = exchange(other_grads, frame_pairs(0, 1))
    same_grads, query_pad = attend_final_call(
        same_keys, query_t, grad_t, totals, partial_t, head_dim
    )
    summed = same_grads.astype(F32) + moved.astype(F32)
    step_rows = block.shape[0]
    low = summed.astype(BF16)
    pieces = [
        exchange(low[s * step_rows : (s + 1) * step_rows], frame_pairs(s, 0))
        for s in range(1, outer)
    ]
    query_back, query_here, query_away = query_side_call(
        place, query_pad, tokens_t, head_dim, count
    )
    query_moved = exchange(query_away, frame_pairs(0, 1))
    pieces, query_back, query_here = lax.optimization_barrier((pieces, query_back, query_here))
    swapped = add_all(summed[:step_rows], pieces).astype(BF16)
    beside = exchange(swapped, outer_pairs(-1))
    mine = exchange(swapped, frame_pairs(0, 1))
    block_rows = 2 * local // count
    padded = round_up(block_rows, 8)
    query_own, query_pieces = scatter_weights(query_here, query_moved, padded)
    beside, mine, query_pieces = lax.optimization_barrier((beside, mine, query_pieces))
    here, away, near, far = pull_call(
        place, mine, swapped, beside, windows, taps, tokens_t, weights, query_back, rows, cols, count
    )
    moved = exchange(away, frame_pairs(0, 1))
    query_sum = add_all(query_own, query_pieces)[:block_rows, :local]
    input_grad = (near + across(far)[:, :local].astype(F32)).astype(BF16)
    own_sum, pieces = scatter_weights(here, moved, padded)
    pieces, input_grad, query_sum = lax.optimization_barrier((pieces, input_grad, query_sum))
    total = add_all(own_sum, pieces)
    weight_grad = jnp.stack([query_sum, total[:block_rows, :local], total[:block_rows, local:]])
    tail = total[padded : padded + 27]
    kernel_grad = jnp.stack([tail[:, :local], tail[:, local:]])
    return input_grad.reshape(tokens.shape), weight_grad, kernel_grad


def solution(mesh):
    in_specs = (
        P(("clips", "frames"), None, None, "heads"),
        P(("clips", "frames"), None, None, "heads"),
        P(None, None, "heads"),
        P(None, None, "heads"),
    )
    out_specs = (
        P(("clips", "frames"), None, None, "heads"),
        P("clips", "frames", "heads"),
        P("clips", None, "heads"),
    )
    return jax.shard_map(shards, mesh=mesh, in_specs=in_specs, out_specs=out_specs, check_vma=False)
```

```python
import functools
import math

import jax
import jax.numpy as jnp
from jax import lax
from jax.experimental import pallas as pl
from jax.experimental.pallas import tpu as pltpu
from jax.sharding import PartitionSpec as P

HEADS = 8
LANES = 128
F32 = jnp.float32
BF16 = jnp.bfloat16
PARAMS = pltpu.CompilerParams(vmem_limit_bytes=16 * 1024 * 1024)
NN = (((1,), (0,)), ((), ()))
NT = (((1,), (1,)), ((), ()))
TN = (((0,), (0,)), ((), ()))


def mul(left, right, dims=NN):
    return lax.dot_general(left, right, dims, preferred_element_type=F32)


def near_core(*arrays):
    return tuple(pltpu.with_memory_space_constraint(x, pltpu.VMEM) for x in arrays)


def vmem():
    return pl.BlockSpec(memory_space=pltpu.VMEM)


def smem():
    return pl.BlockSpec(memory_space=pltpu.SMEM)


def lane_tiles(channels):
    return [
        (k, k * LANES, min(LANES, channels - k * LANES)) for k in range(pl.cdiv(channels, LANES))
    ]


def round_up(size, step):
    return pl.cdiv(size, step) * step


def join_taps(taps, joint):
    local = taps.shape[2]
    for side in range(2):
        joint[0:27, side * local : (side + 1) * local] = taps[:, side, :]


def pool_body(
    geometry, place, own, other, weights, taps, to_pair, to_next, inner, stored, windows, joint, wide
):
    rows, cols, local = geometry
    pooled_rows, pooled_cols = rows // 4, cols // 4
    even = place[0] % 2 == 0
    first = place[1] == 0
    mine, theirs = own[:, :local].astype(F32), other[:, :local].astype(F32)
    low_half = jnp.where(first, mine, theirs)
    high_half = jnp.where(first, theirs, mine)
    tokens = jnp.concatenate([low_half, high_half], axis=1).astype(BF16)
    join_taps(taps, joint)
    starts = lax.broadcasted_iota(jnp.int32, (pooled_cols, LANES), 0) == 0
    both = weights[1:3].reshape(2 * local, 2 * local)
    full = mul(tokens, both, NT).astype(BF16).astype(F32)
    for tile, low, width in lane_tiles(2 * local):
        wide[tile, 0:8, :] = jnp.zeros((8, LANES), F32)
        wide[tile, 8:, :width] = full[:, low : low + width]
        for b in range(3):
            for e in range(3):
                for i in range(pooled_rows):
                    row = 4 * i + b - 1
                    if row < 0:
                        piece = jnp.zeros((pooled_cols, LANES), F32)
                    else:
                        piece = wide[tile, pl.ds(row * cols + e + 7, pooled_cols, stride=4), :]
                        if e == 0:
                            piece = jnp.where(starts, 0.0, piece)
                    at = slice(i * pooled_cols, (i + 1) * pooled_cols)
                    windows[3 * b + e, at, low : low + width] = piece[:, :width]
    for k in range(9):
        stored[k] = windows[k].astype(BF16)
    sums = []
    for a in range(3):
        total = windows[0] * joint[9 * a : 9 * a + 1, :]
        for k in range(1, 9):
            total = total + windows[k] * joint[9 * a + k : 9 * a + k + 1, :]
        sums.append(total)
    earlier, center, later = sums
    to_pair[...] = center.astype(BF16)
    to_next[...] = jnp.where(even, later, earlier).astype(BF16)
    inner[...] = jnp.where(even, earlier, later)


def pool_call(place, own, other, weights, taps, rows, cols):
    both = weights.shape[2]
    count = rows * cols // 16
    return pl.pallas_call(
        functools.partial(pool_body, (rows, cols, both // 2)),
        out_shape=(
            pltpu.VMEM((count, both), BF16),
            pltpu.VMEM((count, both), BF16),
            pltpu.VMEM((count, both), F32),
            jax.ShapeDtypeStruct((9, count, both), BF16),
        ),
        in_specs=[smem()] + [vmem()] * 4,
        out_specs=(vmem(),) * 4,
        scratch_shapes=[
            pltpu.VMEM((9, count, both), F32),
            pltpu.VMEM((32, both), F32),
            pltpu.VMEM((pl.cdiv(both, LANES), rows * cols + 8, LANES), F32),
        ],
        compiler_params=PARAMS,
        name="project_pool",
    )(place, *near_core(own, other), weights, taps)


def spread_rows(head_dim, local, heads):
    rows = lax.broadcasted_iota(jnp.int32, (heads * LANES, local), 0)
    cols = lax.broadcasted_iota(jnp.int32, (heads * LANES, local), 1)
    chosen = rows < 0
    for h in range(heads):
        inside = (cols >= h * head_dim) & (cols < (h + 1) * head_dim)
        chosen = chosen | (inside & (rows == cols + h * (LANES - head_dim)))
    return chosen.astype(F32).astype(BF16)


def identity(size):
    rows = lax.broadcasted_iota(jnp.int32, (size, size), 0)
    cols = lax.broadcasted_iota(jnp.int32, (size, size), 1)
    return (rows == cols).astype(F32).astype(BF16)


def turn_body(geometry, out_grad, grad_t):
    head_dim, local, heads = geometry
    grad_t[...] = mul(spread_rows(head_dim, local, heads), out_grad[...], NT).astype(BF16)


def turn_call(out_grad, head_dim):
    tokens, local = out_grad.shape
    heads = local // head_dim
    return pl.pallas_call(
        functools.partial(turn_body, (head_dim, local, heads)),
        out_shape=pltpu.VMEM((heads * LANES, tokens), BF16),
        in_specs=[vmem()],
        out_specs=vmem(),
        compiler_params=PARAMS,
        name="turn_grad",
    )(out_grad)


def query_body(geometry, place, own, other, weights, query_t, tokens_t):
    head_dim, local, heads = geometry
    spread = spread_rows(head_dim, local, heads)
    turn = identity(local)
    near = pl.multiple_of(place[1] * local, 16)
    far = pl.multiple_of((1 - place[1]) * local, 16)
    tokens_t[pl.ds(near, local), :] = mul(turn, own[:, :local], NT).astype(BF16)
    tokens_t[pl.ds(far, local), :] = mul(turn, other[:, :local], NT).astype(BF16)
    query_t[...] = mul(mul(spread, weights[0]).astype(BF16), tokens_t[...]).astype(BF16)


def query_call(place, own, other, weights, head_dim):
    tokens, local = own.shape[0], weights.shape[1]
    heads = local // head_dim
    return pl.pallas_call(
        functools.partial(query_body, (head_dim, local, heads)),
        out_shape=(
            pltpu.VMEM((heads * LANES, tokens), BF16),
            pltpu.VMEM((2 * local, tokens), BF16),
        ),
        in_specs=[smem()] + [vmem()] * 3,
        out_specs=(vmem(),) * 2,
        compiler_params=PARAMS,
        name="project_query",
    )(place, *near_core(own, other), weights)


def choose_head(head_dim, local, head):
    rows = lax.broadcasted_iota(jnp.int32, (2 * local, 2 * LANES), 0)
    cols = lax.broadcasted_iota(jnp.int32, (2 * local, 2 * LANES), 1)
    lane = cols % LANES
    source = lane + (cols // LANES) * local + head * head_dim
    return ((rows == source) & (lane < head_dim)).astype(F32).astype(BF16)


def head_products(head_dim, keys, chosen, query, grad):
    both = jnp.concatenate([mul(part[...], chosen) for part in keys], axis=0).astype(BF16)
    key, value = both[:, :LANES], both[:, LANES:]
    factor = head_dim ** (-0.5) * math.log2(math.e)
    raised = jnp.exp2(mul(key, query) * factor)
    return key, raised, mul(value, grad)


def measure_body(
    geometry, first, rest, query_t, grad_t, sums, raised_out, prob_grad_out, key_pad
):
    head_dim, local, heads = geometry
    chosen = choose_head(head_dim, local, pl.program_id(0))
    key, raised, prob_grad = head_products(
        head_dim, (first, rest), chosen, query_t[...], grad_t[...]
    )
    raised_out[0] = raised
    prob_grad_out[0] = prob_grad
    key_pad[...] = key
    sums[0, 0:1, :] = jnp.sum(raised, axis=0, keepdims=True)
    sums[0, 1:2, :] = jnp.sum(raised * prob_grad, axis=0, keepdims=True)


def attend_body(geometry, final, *refs):
    head_dim, local, heads = geometry
    head = pl.program_id(0)
    scale = head_dim ** (-0.5)
    chosen = choose_head(head_dim, local, head)
    if final:
        own_raised, own_prob_grad, own_pad, query_t, grad_t, sums, *refs = refs
        other_pad, other_scores, first_grads, rest_grads, query_grad, total = refs
        query, grad = query_t[...], grad_t[...]
        key, raised, prob_grad = own_pad[...], own_raised[0], own_prob_grad[0]
        inverse, centre = sums[0, 0:1, :], sums[0, 1:2, :]
    else:
        first, rest, query_t, grad_t, sums, *refs = refs
        first_grads, rest_grads, key_pad, score_grads, totals, total = refs
        query, grad = query_t[...], grad_t[...]
        key, raised, prob_grad = head_products(head_dim, (first, rest), chosen, query, grad)
        inverse = 1.0 / (sums[0, 0:1, :] + jnp.sum(raised, axis=0, keepdims=True))
        weighted = sums[0, 1:2, :] + jnp.sum(raised * prob_grad, axis=0, keepdims=True)
        centre = weighted * inverse
        totals[0, 0:1, :] = inverse
        totals[0, 1:2, :] = centre
    probs = raised * inverse
    score_grad = (probs * (prob_grad - centre) * scale).astype(BF16)
    if final:
        turn = identity(LANES)
        back_t = grad.astype(F32)
        for keys, scores in ((key, score_grad), (other_pad[...], other_scores[0])):
            back_t = back_t + mul(mul(turn, keys, NT).astype(BF16), scores)
        query_grad[...] = back_t.T.astype(BF16)
    else:
        key_pad[...] = key
        score_grads[0] = score_grad
    value_back = mul(probs.astype(BF16), grad, NT)
    key_back = mul(score_grad, query, NT)
    joined = jnp.concatenate([key_back, value_back], axis=1).astype(BF16)
    placed = mul(joined, chosen, NT)

    @pl.when(head == 0)
    def _():
        total[...] = placed

    @pl.when(head > 0)
    def _():
        total[...] += placed

    @pl.when(head == heads - 1)
    def _():
        split = first_grads.shape[0]
        first_grads[...] = total[:split, :].astype(BF16)
        rest_grads[...] = total[split:, :].astype(BF16)


def whole_spec(array):
    return pl.BlockSpec(array.shape, lambda h: (0,) * len(array.shape))


def head_specs(tokens, key_count):
    rows = pl.BlockSpec((LANES, tokens), lambda h: (h, 0))
    sums = pl.BlockSpec((1, 8, tokens), lambda h: (h, 0, 0))
    keys = pl.BlockSpec((key_count, LANES), lambda h: (0, h))
    scores = pl.BlockSpec((1, key_count, tokens), lambda h: (h, 0, 0))
    return rows, sums, keys, scores


def measure_call(first, rest, query_t, grad_t, head_dim):
    local, tokens = first.shape[1] // 2, query_t.shape[1]
    heads = local // head_dim
    key_count = first.shape[0] + rest.shape[0]
    row_spec, sum_spec, key_spec, score_spec = head_specs(tokens, key_count)
    return pl.pallas_call(
        functools.partial(measure_body, (head_dim, local, heads)),
        grid=(heads,),
        out_shape=(
            pltpu.VMEM((heads, 8, tokens), F32),
            pltpu.VMEM((heads, key_count, tokens), F32),
            pltpu.VMEM((heads, key_count, tokens), F32),
            pltpu.VMEM((key_count, heads * LANES), BF16),
        ),
        in_specs=[whole_spec(first), whole_spec(rest), row_spec, row_spec],
        out_specs=(sum_spec, score_spec, score_spec, key_spec),
        compiler_params=PARAMS,
        name="attend_measure",
    )(*near_core(first, rest, query_t, grad_t))


def attend_call(first, rest, query_t, grad_t, sums, head_dim):
    key_count, both = first.shape[0] + rest.shape[0], first.shape[1]
    local, tokens = both // 2, query_t.shape[1]
    heads = local // head_dim
    row_spec, sum_spec, key_spec, score_spec = head_specs(tokens, key_count)
    return pl.pallas_call(
        functools.partial(attend_body, (head_dim, local, heads), False),
        grid=(heads,),
        out_shape=(
            pltpu.VMEM(first.shape, BF16),
            pltpu.VMEM(rest.shape, BF16),
            pltpu.VMEM((key_count, heads * LANES), BF16),
            pltpu.VMEM((heads, key_count, tokens), BF16),
            pltpu.VMEM((heads, 8, tokens), F32),
        ),
        in_specs=[whole_spec(first), whole_spec(rest), row_spec, row_spec, sum_spec],
        out_specs=(whole_spec(first), whole_spec(rest), key_spec, score_spec, sum_spec),
        scratch_shapes=[pltpu.VMEM((key_count, both), F32)],
        compiler_params=PARAMS,
        name="attend_other",
    )(*near_core(first, rest, query_t, grad_t, sums))


def attend_final_call(saved, query_t, grad_t, totals, extra, head_dim, local, split):
    key_count, tokens = saved[0].shape[1:]
    heads = local // head_dim
    row_spec, sum_spec, key_spec, score_spec = head_specs(tokens, key_count)
    shapes = ((split, 2 * local), (key_count - split, 2 * local))
    outs = [pltpu.VMEM(shape, BF16) for shape in shapes]
    specs = [pl.BlockSpec(shape, lambda h: (0, 0)) for shape in shapes]
    in_specs = [score_spec, score_spec, key_spec, row_spec, row_spec, sum_spec]
    return pl.pallas_call(
        functools.partial(attend_body, (head_dim, local, heads), True),
        grid=(heads,),
        out_shape=(*outs, pltpu.VMEM((tokens, heads * LANES), BF16)),
        in_specs=[*in_specs, key_spec, score_spec],
        out_specs=(*specs, pl.BlockSpec((tokens, LANES), lambda h: (0, h))),
        scratch_shapes=[pltpu.VMEM((key_count, 2 * local), F32)],
        compiler_params=PARAMS,
        name="attend_same",
    )(*near_core(*saved, query_t, grad_t, totals, *extra))


def store_blocks(position, count, rows, column, here, away, away_own=None):
    padded = round_up(rows, 8)
    width = column.shape[1]
    for j in range(count):
        relative = position ^ j
        outer = relative // 2
        value = column[j * rows : (j + 1) * rows, :]

        @pl.when(relative % 2 == 0)
        def _(value=value, outer=outer):
            here[pl.ds(pl.multiple_of(outer * padded, 8), rows), :width] = value

        if away_own is None:

            @pl.when(relative % 2 == 1)
            def _(value=value, outer=outer):
                at = pl.multiple_of(outer * padded, 8)
                away[pl.ds(at, rows), :width] = value.astype(BF16)

        else:

            @pl.when(relative == 1)
            def _(value=value):
                away_own[:rows, :width] = value.astype(BF16)

            @pl.when((relative % 2 == 1) & (relative > 1))
            def _(value=value, outer=outer):
                at = pl.multiple_of((outer - 1) * padded, 8)
                away[pl.ds(at, rows), :width] = value.astype(BF16)


def query_side_body(geometry, place, query_pad, tokens_t, query_back, here, away):
    head_dim, local, heads, count = geometry
    spread = spread_rows(head_dim, local, heads)
    back = mul(query_pad[...], spread).astype(BF16)
    query_back[...] = back
    here[...] = jnp.zeros(here.shape, F32)
    away[...] = jnp.zeros(away.shape, BF16)
    column = mul(tokens_t[...], back)
    store_blocks(place[0], count, 2 * local // count, column, here, away)


def query_side_call(place, query_pad, tokens_t, head_dim, count):
    both, tokens = tokens_t.shape
    local = both // 2
    shape = (count // 2 * round_up(both // count, 8), round_up(local, LANES))
    return pl.pallas_call(
        functools.partial(query_side_body, (head_dim, local, local // head_dim, count)),
        out_shape=(
            pltpu.VMEM((tokens, local), BF16),
            pltpu.VMEM(shape, F32),
            pltpu.VMEM(shape, BF16),
        ),
        in_specs=[smem()] + [vmem()] * 2,
        out_specs=(vmem(),) * 3,
        compiler_params=PARAMS,
        name="query_side",
    )(place, *near_core(query_pad, tokens_t))


def pull_body(
    geometry,
    place,
    mine,
    swapped,
    beside,
    windows,
    taps,
    tokens_t,
    weights,
    query_back,
    here,
    away,
    away_own,
    token_near,
    token_far,
    wide,
    staged,
    joint,
    folded,
):
    rows, cols, local, count = geometry
    pooled_rows, pooled_cols = rows // 4, cols // 4
    position = place[0]
    even = position % 2 == 0
    pooled = pooled_rows * pooled_cols
    block_rows = 2 * local // count
    padded = round_up(block_rows, 8)
    outer = count // 2
    join_taps(taps, joint)
    starts = lax.broadcasted_iota(jnp.int32, (pooled, 2 * local), 0) % pooled_cols == 0
    folded[...] = jnp.zeros(folded.shape, F32)
    wide[...] = jnp.zeros(wide.shape, F32)
    if padded > block_rows:
        here[...] = jnp.zeros(here.shape, F32)
        away[...] = jnp.zeros(away.shape, BF16)
        away_own[...] = jnp.zeros(away_own.shape, BF16)
    partner, distant = swapped[...].astype(F32), beside[...].astype(F32)
    grads = [
        jnp.where(even, partner, distant),
        mine[...].astype(F32),
        jnp.where(even, distant, partner),
    ]
    for b in range(3):
        for e in range(3):
            k = 3 * b + e
            window = windows[k].astype(F32)
            spread = None
            for a in range(3):
                term = grads[a] * joint[9 * a + k : 9 * a + k + 1, :]
                spread = term if spread is None else spread + term
                folded[9 * a + k : 9 * a + k + 1, :] = jnp.sum(
                    grads[a] * window, axis=0, keepdims=True
                )
            if e == 0:
                spread = jnp.where(starts, 0.0, spread)
            for tile, low, width in lane_tiles(2 * local):
                staged[tile, :, :width] = spread[:, low : low + width]
                for i in range(pooled_rows):
                    row = 4 * i + b - 1
                    if row >= 0:
                        at = slice(i * pooled_cols, (i + 1) * pooled_cols)
                        wide[tile, pl.ds(row * cols + e + 7, pooled_cols, stride=4), :] = staged[
                            tile, at, :
                        ]
    back = jnp.concatenate(
        [wide[tile, 8:, :width] for tile, low, width in lane_tiles(2 * local)], axis=1
    ).astype(BF16)
    column = mul(tokens_t[...], back)
    here[outer * padded :, :] = folded[...]
    away[(outer - 1) * padded :, :] = folded[...].astype(BF16)
    store_blocks(position, count, block_rows, column, here, away, away_own)
    both = weights[1:3].reshape(2 * local, 2 * local)
    token_sum = mul(query_back[...], weights[0]) + mul(back, both)
    first = place[1] == 0
    low_half, high_half = token_sum[:, :local], token_sum[:, local:]
    token_near[...] = jnp.where(first, low_half, high_half)
    token_far[:, :local] = jnp.where(first, high_half, low_half).astype(BF16)
    token_far[:, local:] = jnp.zeros((token_far.shape[0], token_far.shape[1] - local), BF16)


def pull_call(
    place, mine, swapped, beside, windows, taps, tokens_t, weights, query_back, rows, cols, count
):
    both, tokens = tokens_t.shape
    local = both // 2
    padded = round_up(both // count, 8)
    size = count // 2 * padded + 32
    tiles = pl.cdiv(both, LANES)
    return pl.pallas_call(
        functools.partial(pull_body, (rows, cols, local, count)),
        out_shape=(
            pltpu.VMEM((size, both), F32),
            pltpu.VMEM((size - padded, both), BF16),
            pltpu.VMEM((padded, both), BF16),
            pltpu.VMEM((tokens, local), F32),
            pltpu.VMEM((tokens, round_up(local, LANES)), BF16),
        ),
        in_specs=[smem()] + [vmem()] * 8,
        out_specs=(vmem(),) * 5,
        scratch_shapes=[
            pltpu.VMEM((tiles, tokens + 8, LANES), F32),
            pltpu.VMEM((tiles, rows * cols // 16, LANES), F32),
            pltpu.VMEM((32, both), F32),
            pltpu.VMEM((32, both), F32),
        ],
        compiler_params=PARAMS,
        name="pull_back",
    )(
        place,
        *near_core(mine, swapped, beside),
        windows,
        taps,
        *near_core(tokens_t),
        weights,
        *near_core(query_back),
    )


def finish_body(rows, query_sum, own_sum, tail_sum, *refs):
    *pieces, weight_grad, kernel_grad = refs
    local = weight_grad.shape[2]
    padded = own_sum.shape[0]
    total, tail = own_sum[...], tail_sum[...]
    for piece in pieces:
        total = total + piece[:padded, :].astype(F32)
        tail = tail + piece[padded:, :].astype(F32)
    weight_grad[0] = query_sum[:rows, :local]
    weight_grad[1] = total[:rows, :local]
    weight_grad[2] = total[:rows, local:]
    for side in range(2):
        for k in range(kernel_grad.shape[0]):
            kernel_grad[k, side : side + 1, :] = tail[k : k + 1, side * local : (side + 1) * local]


def finish_call(query_sum, own_sum, tail_sum, pieces, rows, local):
    return pl.pallas_call(
        functools.partial(finish_body, rows),
        out_shape=(
            jax.ShapeDtypeStruct((3, rows, local), F32),
            jax.ShapeDtypeStruct((27, 2, local), F32),
        ),
        in_specs=[vmem()] * (3 + len(pieces)),
        out_specs=(vmem(),) * 2,
        compiler_params=PARAMS,
        name="finish",
    )(*near_core(query_sum, own_sum, tail_sum, *pieces))


def frame_pairs(step, flip):
    count = lax.axis_size("frames")
    return [(i, i ^ (2 * step + flip)) for i in range(count)]


def outer_pairs(direction):
    count = lax.axis_size("frames")
    moves = [(i, i + direction * (2 if i % 2 else -2)) for i in range(count)]
    return [(i, j) for i, j in moves if 0 <= j < count]


def exchange(block, pairs):
    return lax.ppermute(block, "frames", pairs)


def across(block):
    return lax.ppermute(block, "heads", [(0, 1), (1, 0)])


def scatter_weights(here, moved, rows):
    outer = lax.axis_size("frames") // 2
    summed = here + moved.astype(F32)
    end = outer * rows
    own = jnp.concatenate([summed[:rows], summed[end:]])
    low = summed.astype(BF16)
    pieces = []
    for step in range(1, outer):
        piece = jnp.concatenate([low[step * rows : (step + 1) * rows], low[end:]])
        pieces.append(exchange(piece, frame_pairs(step, 0)))
    return own, pieces


def add_all(own, pieces):
    for piece in pieces:
        own = own + piece.astype(F32)
    return own


def shards(tokens, out_grad, w_qkv, pool_kernel):
    local = tokens.shape[-1]
    heads_here = HEADS // lax.axis_size("heads")
    head_dim = local // heads_here
    rows, cols = tokens.shape[1], tokens.shape[2]
    token_count = rows * cols
    count = lax.axis_size("frames")
    frame = lax.axis_index("frames")
    core = lax.axis_index("heads")
    place = jnp.stack([frame, core]).astype(jnp.int32)
    outer = count // 2
    spare = round_up(local, LANES) - local
    own = jnp.pad(tokens.reshape(token_count, local), ((0, 0), (0, spare)))
    grad = out_grad.reshape(token_count, local)
    across_pair, barrier = frame_pairs(0, 1), lax.optimization_barrier
    other = across(own)
    grad_t = turn_call(grad, head_dim)
    other, grad_t = barrier((other, grad_t))
    weights = w_qkv.transpose(0, 2, 1)
    taps = pool_kernel.transpose(1, 0, 2)
    to_pair, to_next, inner, windows = pool_call(place, own, other, weights, taps, rows, cols)
    from_next = exchange(to_next, outer_pairs(1))
    from_pair = exchange(to_pair, across_pair)
    block = (inner + from_pair.astype(F32) + from_next.astype(F32)).astype(BF16)
    others = [exchange(block, frame_pairs(s, 0)) for s in range(1, outer)]
    other_first = exchange(block, across_pair)
    block, own, other = barrier((block, own, other))
    query_t, tokens_t = query_call(place, own, other, weights, head_dim)
    others, other_first, query_t, grad_t, tokens_t = barrier(
        (others, other_first, query_t, grad_t, tokens_t)
    )
    same_rest = jnp.concatenate(others)
    other_rest = exchange(same_rest, across_pair)
    sums, *saved = measure_call(block, same_rest, query_t, grad_t, head_dim)
    first_other, rest_other, *for_other, totals = attend_call(
        other_first, other_rest, query_t, grad_t, sums, head_dim
    )
    rest_moved = exchange(rest_other, across_pair)
    step_rows = block.shape[0]
    first_same, rest_same, query_pad = attend_final_call(
        saved, query_t, grad_t, totals, for_other, head_dim, local, step_rows
    )
    rest_moved, first_other = barrier((rest_moved, first_other))
    low = (rest_same.astype(F32) + rest_moved.astype(F32)).astype(BF16)
    pieces = [
        exchange(low[(s - 1) * step_rows : s * step_rows], frame_pairs(s, 0))
        for s in range(1, outer)
    ]
    first_moved = exchange(first_other, across_pair)
    query_back, query_here, query_away = query_side_call(
        place, query_pad, tokens_t, head_dim, count
    )
    pieces, first_moved, query_back, query_here, query_away = barrier(
        (pieces, first_moved, query_back, query_here, query_away)
    )
    summed = first_same.astype(F32) + first_moved.astype(F32)
    swapped = add_all(summed, pieces).astype(BF16)
    beside = exchange(swapped, outer_pairs(-1))
    mine = exchange(swapped, frame_pairs(0, 1))
    beside, mine, query_away = barrier((beside, mine, query_away))
    query_moved = exchange(query_away, across_pair)
    block_rows = 2 * local // count
    padded = round_up(block_rows, 8)
    here, away, away_own, near, far = pull_call(
        place, mine, swapped, beside, windows, taps, tokens_t, weights, query_back, rows, cols, count
    )
    moved = exchange(away, frame_pairs(0, 1))
    query_moved, near, far = barrier((query_moved, near, far))
    query_own, query_pieces = scatter_weights(query_here, query_moved, padded)
    moved, query_pieces = barrier((moved, query_pieces))
    query_sum = add_all(query_own, query_pieces)
    input_grad = (near + across(far)[:, :local].astype(F32)).astype(BF16)
    rest_sum = here[padded:] + moved.astype(F32)
    low, end = rest_sum.astype(BF16), (outer - 1) * padded
    pieces = [
        exchange(
            jnp.concatenate([low[(s - 1) * padded : s * padded], low[end:]]), frame_pairs(s, 0)
        )
        for s in range(1, outer)
    ]
    own_moved = exchange(barrier((away_own, moved))[0], across_pair)
    own_sum, tail_sum = here[:padded] + own_moved.astype(F32), rest_sum[end:]
    pieces, input_grad, query_sum, own_sum, tail_sum = barrier(
        (pieces, input_grad, query_sum, own_sum, tail_sum)
    )
    weight_grad, kernel_grad = finish_call(
        query_sum, own_sum, tail_sum, pieces, block_rows, local
    )
    return input_grad.reshape(tokens.shape), weight_grad, kernel_grad.transpose(1, 0, 2)


def solution(mesh):
    in_specs = (
        P(("clips", "frames"), None, None, "heads"),
        P(("clips", "frames"), None, None, "heads"),
        P(None, None, "heads"),
        P(None, None, "heads"),
    )
    out_specs = (
        P(("clips", "frames"), None, None, "heads"),
        P("clips", "frames", "heads"),
        P("clips", None, "heads"),
    )
    return jax.shard_map(shards, mesh=mesh, in_specs=in_specs, out_specs=out_specs, check_vma=False)
```

```python
import functools
import math

import jax
import jax.numpy as jnp
from jax import lax
from jax.experimental import pallas as pl
from jax.experimental.pallas import tpu as pltpu
from jax.sharding import PartitionSpec as P

HEADS = 8
LANES = 128
STEP = 4
F32 = jnp.float32
BF16 = jnp.bfloat16
PARAMS = pltpu.CompilerParams(vmem_limit_bytes=24 * 1024 * 1024)
NN = (((1,), (0,)), ((), ()))
NT = (((1,), (1,)), ((), ()))
TN = (((0,), (0,)), ((), ()))


def mul(left, right, dims=NN):
    return lax.dot_general(left, right, dims, preferred_element_type=F32)


def near_core(*arrays):
    return tuple(pltpu.with_memory_space_constraint(x, pltpu.VMEM) for x in arrays)


def vmem():
    return pl.BlockSpec(memory_space=pltpu.VMEM)


def smem():
    return pl.BlockSpec(memory_space=pltpu.SMEM)


def lane_tiles(channels):
    return [
        (k, k * LANES, min(LANES, channels - k * LANES)) for k in range(pl.cdiv(channels, LANES))
    ]


def round_up(size, step):
    return pl.cdiv(size, step) * step


def join_taps(taps, joint):
    local = taps.shape[2]
    for side in range(2):
        joint[0:27, side * local : (side + 1) * local] = taps[:, side, :]


def pool_body(
    geometry, place, own, other, weights, taps, to_pair, to_next, inner, stored, windows, joint, wide
):
    rows, cols, local = geometry
    pooled_rows, pooled_cols = rows // 4, cols // 4
    even = place[0] % 2 == 0
    first = place[1] == 0
    mine, theirs = own[:, :local].astype(F32), other[:, :local].astype(F32)
    low_half = jnp.where(first, mine, theirs)
    high_half = jnp.where(first, theirs, mine)
    tokens = jnp.concatenate([low_half, high_half], axis=1).astype(BF16)
    join_taps(taps, joint)
    starts = lax.broadcasted_iota(jnp.int32, (pooled_cols, LANES), 0) == 0
    both = weights[1:3].reshape(2 * local, 2 * local)
    full = mul(tokens, both, NT).astype(BF16).astype(F32)
    for tile, low, width in lane_tiles(2 * local):
        wide[tile, 0:8, :] = jnp.zeros((8, LANES), F32)
        wide[tile, 8:, :width] = full[:, low : low + width]
        for b in range(3):
            for e in range(3):
                for i in range(pooled_rows):
                    row = 4 * i + b - 1
                    if row < 0:
                        piece = jnp.zeros((pooled_cols, LANES), F32)
                    else:
                        piece = wide[tile, pl.ds(row * cols + e + 7, pooled_cols, stride=4), :]
                        if e == 0:
                            piece = jnp.where(starts, 0.0, piece)
                    at = slice(i * pooled_cols, (i + 1) * pooled_cols)
                    windows[3 * b + e, at, low : low + width] = piece[:, :width]
    for k in range(9):
        stored[k] = windows[k].astype(BF16)
    sums = []
    for a in range(3):
        total = windows[0] * joint[9 * a : 9 * a + 1, :]
        for k in range(1, 9):
            total = total + windows[k] * joint[9 * a + k : 9 * a + k + 1, :]
        sums.append(total)
    earlier, center, later = sums
    to_pair[...] = center.astype(BF16)
    to_next[...] = jnp.where(even, later, earlier).astype(BF16)
    inner[...] = jnp.where(even, earlier, later)


def pool_call(place, own, other, weights, taps, rows, cols):
    both = weights.shape[2]
    count = rows * cols // 16
    return pl.pallas_call(
        functools.partial(pool_body, (rows, cols, both // 2)),
        out_shape=(
            pltpu.VMEM((count, both), BF16),
            pltpu.VMEM((count, both), BF16),
            pltpu.VMEM((count, both), F32),
            jax.ShapeDtypeStruct((9, count, both), BF16),
        ),
        in_specs=[smem()] + [vmem()] * 4,
        out_specs=(vmem(),) * 4,
        scratch_shapes=[
            pltpu.VMEM((9, count, both), F32),
            pltpu.VMEM((32, both), F32),
            pltpu.VMEM((pl.cdiv(both, LANES), rows * cols + 8, LANES), F32),
        ],
        compiler_params=PARAMS,
        name="project_pool",
    )(place, *near_core(own, other), weights, taps)


def spread_rows(head_dim, local, heads):
    rows = lax.broadcasted_iota(jnp.int32, (heads * LANES, local), 0)
    cols = lax.broadcasted_iota(jnp.int32, (heads * LANES, local), 1)
    chosen = rows < 0
    for h in range(heads):
        inside = (cols >= h * head_dim) & (cols < (h + 1) * head_dim)
        chosen = chosen | (inside & (rows == cols + h * (LANES - head_dim)))
    return chosen.astype(F32).astype(BF16)


def identity(size):
    rows = lax.broadcasted_iota(jnp.int32, (size, size), 0)
    cols = lax.broadcasted_iota(jnp.int32, (size, size), 1)
    return (rows == cols).astype(F32).astype(BF16)


def turn_body(geometry, out_grad, grad_t):
    head_dim, local, heads = geometry
    grad_t[...] = mul(spread_rows(head_dim, local, heads), out_grad[...], NT).astype(BF16)


def turn_call(out_grad, head_dim):
    tokens, local = out_grad.shape
    heads = local // head_dim
    return pl.pallas_call(
        functools.partial(turn_body, (head_dim, local, heads)),
        out_shape=pltpu.VMEM((heads * LANES, tokens), BF16),
        in_specs=[vmem()],
        out_specs=vmem(),
        compiler_params=PARAMS,
        name="turn_grad",
    )(out_grad)


def query_body(geometry, place, own, other, weights, query_t, tokens_t):
    head_dim, local, heads = geometry
    spread = spread_rows(head_dim, local, heads)
    turn = identity(local)
    near = pl.multiple_of(place[1] * local, 16)
    far = pl.multiple_of((1 - place[1]) * local, 16)
    tokens_t[pl.ds(near, local), :] = mul(turn, own[:, :local], NT).astype(BF16)
    tokens_t[pl.ds(far, local), :] = mul(turn, other[:, :local], NT).astype(BF16)
    query_t[...] = mul(mul(spread, weights[0]).astype(BF16), tokens_t[...]).astype(BF16)


def query_call(place, own, other, weights, head_dim):
    tokens, local = own.shape[0], weights.shape[1]
    heads = local // head_dim
    return pl.pallas_call(
        functools.partial(query_body, (head_dim, local, heads)),
        out_shape=(
            pltpu.VMEM((heads * LANES, tokens), BF16),
            pltpu.VMEM((2 * local, tokens), BF16),
        ),
        in_specs=[smem()] + [vmem()] * 3,
        out_specs=(vmem(),) * 2,
        compiler_params=PARAMS,
        name="project_query",
    )(place, *near_core(own, other), weights)


def choose_head(head_dim, local, head):
    rows = lax.broadcasted_iota(jnp.int32, (2 * local, 2 * LANES), 0)
    cols = lax.broadcasted_iota(jnp.int32, (2 * local, 2 * LANES), 1)
    lane = cols % LANES
    source = lane + (cols // LANES) * local + head * head_dim
    return ((rows == source) & (lane < head_dim)).astype(F32).astype(BF16)


def head_products(head_dim, keys, chosen, query, grad):
    both = jnp.concatenate([mul(part[...], chosen) for part in keys], axis=0).astype(BF16)
    key, value = both[:, :LANES], both[:, LANES:]
    factor = head_dim ** (-0.5) * math.log2(math.e)
    raised = jnp.exp2(mul(key, query) * factor)
    return key, raised, mul(value, grad)


def measure_body(
    geometry, first, rest, query_t, grad_t, sums, raised_out, prob_grad_out, key_pad
):
    head_dim, local, heads = geometry
    for sub in range(STEP):
        rows = slice(sub * LANES, (sub + 1) * LANES)
        chosen = choose_head(head_dim, local, STEP * pl.program_id(0) + sub)
        key, raised, prob_grad = head_products(
            head_dim, (first, rest), chosen, query_t[rows, :], grad_t[rows, :]
        )
        raised_out[sub] = raised
        prob_grad_out[sub] = prob_grad
        key_pad[:, rows] = key
        sums[sub, 0:1, :] = jnp.sum(raised, axis=0, keepdims=True)
        sums[sub, 1:2, :] = jnp.sum(raised * prob_grad, axis=0, keepdims=True)


def attend_body(geometry, final, *refs):
    head_dim, local, heads = geometry
    step = pl.program_id(0)
    scale = head_dim ** (-0.5)
    if final:
        own_raised, own_prob_grad, own_pad, query_t, grad_t, sums, *refs = refs
        other_pad, other_scores, first_grads, rest_grads, query_grad, total = refs
    else:
        first, rest, query_t, grad_t, sums, *refs = refs
        first_grads, rest_grads, key_pad, score_grads, totals, total = refs
    joined, choices = [], []
    for sub in range(STEP):
        rows = slice(sub * LANES, (sub + 1) * LANES)
        chosen = choose_head(head_dim, local, STEP * step + sub)
        query, grad = query_t[rows, :], grad_t[rows, :]
        if final:
            key, raised, prob_grad = own_pad[:, rows], own_raised[sub], own_prob_grad[sub]
            inverse, centre = sums[sub, 0:1, :], sums[sub, 1:2, :]
        else:
            key, raised, prob_grad = head_products(head_dim, (first, rest), chosen, query, grad)
            inverse = 1.0 / (sums[sub, 0:1, :] + jnp.sum(raised, axis=0, keepdims=True))
            weighted = sums[sub, 1:2, :] + jnp.sum(raised * prob_grad, axis=0, keepdims=True)
            centre = weighted * inverse
            totals[sub, 0:1, :] = inverse
            totals[sub, 1:2, :] = centre
        probs = raised * inverse
        score_grad = (probs * (prob_grad - centre) * scale).astype(BF16)
        if final:
            turn = identity(LANES)
            back_t = grad.astype(F32)
            for keys, scores in ((key, score_grad), (other_pad[:, rows], other_scores[sub])):
                back_t = back_t + mul(mul(turn, keys, NT).astype(BF16), scores)
            query_grad[:, rows] = back_t.T.astype(BF16)
        else:
            key_pad[:, rows] = key
            score_grads[sub] = score_grad
        value_back = mul(probs.astype(BF16), grad, NT)
        key_back = mul(score_grad, query, NT)
        joined += [key_back.astype(BF16), value_back.astype(BF16)]
        choices.append(chosen)
    placed = mul(jnp.concatenate(joined, axis=1), jnp.concatenate(choices, axis=1), NT)

    @pl.when(step == 0)
    def _():
        total[...] = placed

    @pl.when(step > 0)
    def _():
        total[...] += placed

    @pl.when(step == heads // STEP - 1)
    def _():
        split = first_grads.shape[0]
        first_grads[...] = total[:split, :].astype(BF16)
        rest_grads[...] = total[split:, :].astype(BF16)


def whole_spec(array):
    return pl.BlockSpec(array.shape, lambda h: (0,) * len(array.shape))


def head_specs(tokens, key_count):
    rows = pl.BlockSpec((STEP * LANES, tokens), lambda h: (h, 0))
    sums = pl.BlockSpec((STEP, 8, tokens), lambda h: (h, 0, 0))
    keys = pl.BlockSpec((key_count, STEP * LANES), lambda h: (0, h))
    scores = pl.BlockSpec((STEP, key_count, tokens), lambda h: (h, 0, 0))
    return rows, sums, keys, scores


def measure_call(first, rest, query_t, grad_t, head_dim):
    local, tokens = first.shape[1] // 2, query_t.shape[1]
    heads = local // head_dim
    key_count = first.shape[0] + rest.shape[0]
    row_spec, sum_spec, key_spec, score_spec = head_specs(tokens, key_count)
    return pl.pallas_call(
        functools.partial(measure_body, (head_dim, local, heads)),
        grid=(heads // STEP,),
        out_shape=(
            pltpu.VMEM((heads, 8, tokens), F32),
            pltpu.VMEM((heads, key_count, tokens), F32),
            pltpu.VMEM((heads, key_count, tokens), F32),
            pltpu.VMEM((key_count, heads * LANES), BF16),
        ),
        in_specs=[whole_spec(first), whole_spec(rest), row_spec, row_spec],
        out_specs=(sum_spec, score_spec, score_spec, key_spec),
        compiler_params=PARAMS,
        name="attend_measure",
    )(*near_core(first, rest, query_t, grad_t))


def attend_call(first, rest, query_t, grad_t, sums, head_dim):
    key_count, both = first.shape[0] + rest.shape[0], first.shape[1]
    local, tokens = both // 2, query_t.shape[1]
    heads = local // head_dim
    row_spec, sum_spec, key_spec, score_spec = head_specs(tokens, key_count)
    return pl.pallas_call(
        functools.partial(attend_body, (head_dim, local, heads), False),
        grid=(heads // STEP,),
        out_shape=(
            pltpu.VMEM(first.shape, BF16),
            pltpu.VMEM(rest.shape, BF16),
            pltpu.VMEM((key_count, heads * LANES), BF16),
            pltpu.VMEM((heads, key_count, tokens), BF16),
            pltpu.VMEM((heads, 8, tokens), F32),
        ),
        in_specs=[whole_spec(first), whole_spec(rest), row_spec, row_spec, sum_spec],
        out_specs=(whole_spec(first), whole_spec(rest), key_spec, score_spec, sum_spec),
        scratch_shapes=[pltpu.VMEM((key_count, both), F32)],
        compiler_params=PARAMS,
        name="attend_other",
    )(*near_core(first, rest, query_t, grad_t, sums))


def attend_final_call(saved, query_t, grad_t, totals, extra, head_dim, local, split):
    key_count, tokens = saved[0].shape[1:]
    heads = local // head_dim
    row_spec, sum_spec, key_spec, score_spec = head_specs(tokens, key_count)
    shapes = ((split, 2 * local), (key_count - split, 2 * local))
    outs = [pltpu.VMEM(shape, BF16) for shape in shapes]
    specs = [pl.BlockSpec(shape, lambda h: (0, 0)) for shape in shapes]
    in_specs = [score_spec, score_spec, key_spec, row_spec, row_spec, sum_spec]
    return pl.pallas_call(
        functools.partial(attend_body, (head_dim, local, heads), True),
        grid=(heads // STEP,),
        out_shape=(*outs, pltpu.VMEM((tokens, heads * LANES), BF16)),
        in_specs=[*in_specs, key_spec, score_spec],
        out_specs=(*specs, pl.BlockSpec((tokens, STEP * LANES), lambda h: (0, h))),
        scratch_shapes=[pltpu.VMEM((key_count, 2 * local), F32)],
        compiler_params=PARAMS,
        name="attend_same",
    )(*near_core(*saved, query_t, grad_t, totals, *extra))


def store_blocks(position, count, rows, column, here, away):
    padded = round_up(rows, 8)
    width = column.shape[1]
    for j in range(count):
        relative = position ^ j
        at = pl.multiple_of((relative // 2) * padded, 8)
        value = column[j * rows : (j + 1) * rows, :]

        @pl.when(relative % 2 == 0)
        def _(value=value, at=at):
            here[pl.ds(at, rows), :width] = value

        @pl.when(relative % 2 == 1)
        def _(value=value, at=at):
            away[pl.ds(at, rows), :width] = value.astype(BF16)


def query_side_body(geometry, place, query_pad, tokens_t, query_back, here, away):
    head_dim, local, heads, count = geometry
    spread = spread_rows(head_dim, local, heads)
    back = mul(query_pad[...], spread).astype(BF16)
    query_back[...] = back
    here[...] = jnp.zeros(here.shape, F32)
    away[...] = jnp.zeros(away.shape, BF16)
    column = mul(tokens_t[...], back)
    store_blocks(place[0], count, 2 * local // count, column, here, away)


def query_side_call(place, query_pad, tokens_t, head_dim, count):
    both, tokens = tokens_t.shape
    local = both // 2
    shape = (count // 2 * round_up(both // count, 8), round_up(local, LANES))
    return pl.pallas_call(
        functools.partial(query_side_body, (head_dim, local, local // head_dim, count)),
        out_shape=(
            pltpu.VMEM((tokens, local), BF16),
            pltpu.VMEM(shape, F32),
            pltpu.VMEM(shape, BF16),
        ),
        in_specs=[smem()] + [vmem()] * 2,
        out_specs=(vmem(),) * 3,
        compiler_params=PARAMS,
        name="query_side",
    )(place, *near_core(query_pad, tokens_t))


def pull_body(
    geometry,
    place,
    mine,
    swapped,
    beside,
    windows,
    taps,
    tokens_t,
    here,
    away,
    backs,
    wide,
    staged,
    joint,
    folded,
):
    rows, cols, local, count = geometry
    pooled_rows, pooled_cols = rows // 4, cols // 4
    position = place[0]
    even = position % 2 == 0
    pooled = pooled_rows * pooled_cols
    block_rows = 2 * local // count
    padded = round_up(block_rows, 8)
    outer = count // 2
    join_taps(taps, joint)
    starts = lax.broadcasted_iota(jnp.int32, (pooled, 2 * local), 0) % pooled_cols == 0
    folded[...] = jnp.zeros(folded.shape, F32)
    wide[...] = jnp.zeros(wide.shape, F32)
    if padded > block_rows:
        here[...] = jnp.zeros(here.shape, F32)
        away[...] = jnp.zeros(away.shape, BF16)
    partner, distant = swapped[...].astype(F32), beside[...].astype(F32)
    grads = [
        jnp.where(even, partner, distant),
        mine[...].astype(F32),
        jnp.where(even, distant, partner),
    ]
    for b in range(3):
        for e in range(3):
            k = 3 * b + e
            window = windows[k].astype(F32)
            spread = None
            for a in range(3):
                term = grads[a] * joint[9 * a + k : 9 * a + k + 1, :]
                spread = term if spread is None else spread + term
                folded[9 * a + k : 9 * a + k + 1, :] = jnp.sum(
                    grads[a] * window, axis=0, keepdims=True
                )
            if e == 0:
                spread = jnp.where(starts, 0.0, spread)
            for tile, low, width in lane_tiles(2 * local):
                staged[tile, :, :width] = spread[:, low : low + width]
                for i in range(pooled_rows):
                    row = 4 * i + b - 1
                    if row >= 0:
                        at = slice(i * pooled_cols, (i + 1) * pooled_cols)
                        wide[tile, pl.ds(row * cols + e + 7, pooled_cols, stride=4), :] = staged[
                            tile, at, :
                        ]
    back = jnp.concatenate(
        [wide[tile, 8:, :width] for tile, low, width in lane_tiles(2 * local)], axis=1
    ).astype(BF16)
    backs[...] = back
    column = mul(tokens_t[...], back)
    here[outer * padded :, :] = folded[...]
    away[outer * padded :, :] = folded[...].astype(BF16)
    store_blocks(position, count, block_rows, column, here, away)


def token_body(place, query_back, backs, weights, token_near, token_far):
    local = weights.shape[1]
    both = weights[1:3].reshape(2 * local, 2 * local)
    token_sum = mul(query_back[...], weights[0]) + mul(backs[...], both)
    first = place[1] == 0
    low_half, high_half = token_sum[:, :local], token_sum[:, local:]
    token_near[...] = jnp.where(first, low_half, high_half)
    token_far[:, :local] = jnp.where(first, high_half, low_half).astype(BF16)
    token_far[:, local:] = jnp.zeros((token_far.shape[0], token_far.shape[1] - local), BF16)


def token_call(place, query_back, backs, weights):
    tokens, local = query_back.shape
    return pl.pallas_call(
        token_body,
        out_shape=(
            pltpu.VMEM((tokens, local), F32),
            pltpu.VMEM((tokens, round_up(local, LANES)), BF16),
        ),
        in_specs=[smem()] + [vmem()] * 3,
        out_specs=(vmem(),) * 2,
        compiler_params=PARAMS,
        name="token_side",
    )(place, *near_core(query_back, backs), weights)


def pull_call(
    place, mine, swapped, beside, windows, taps, tokens_t, rows, cols, count
):
    both, tokens = tokens_t.shape
    local = both // 2
    padded = round_up(both // count, 8)
    size = count // 2 * padded + 32
    tiles = pl.cdiv(both, LANES)
    return pl.pallas_call(
        functools.partial(pull_body, (rows, cols, local, count)),
        out_shape=(
            pltpu.VMEM((size, both), F32),
            pltpu.VMEM((size, both), BF16),
            pltpu.VMEM((tokens, both), BF16),
        ),
        in_specs=[smem()] + [vmem()] * 6,
        out_specs=(vmem(),) * 3,
        scratch_shapes=[
            pltpu.VMEM((tiles, tokens + 8, LANES), F32),
            pltpu.VMEM((tiles, rows * cols // 16, LANES), F32),
            pltpu.VMEM((32, both), F32),
            pltpu.VMEM((32, both), F32),
        ],
        compiler_params=PARAMS,
        name="pull_back",
    )(
        place,
        *near_core(mine, swapped, beside),
        windows,
        taps,
        *near_core(tokens_t),
    )


def finish_body(rows, query_sum, own_sum, tail_sum, *refs):
    *pieces, weight_grad, kernel_grad = refs
    local = weight_grad.shape[2]
    padded = own_sum.shape[0]
    total, tail = own_sum[...], tail_sum[...]
    for piece in pieces:
        total = total + piece[:padded, :].astype(F32)
        tail = tail + piece[padded:, :].astype(F32)
    weight_grad[0] = query_sum[:rows, :local]
    weight_grad[1] = total[:rows, :local]
    weight_grad[2] = total[:rows, local:]
    for side in range(2):
        for k in range(kernel_grad.shape[0]):
            kernel_grad[k, side : side + 1, :] = tail[k : k + 1, side * local : (side + 1) * local]


def finish_call(query_sum, own_sum, tail_sum, pieces, rows, local):
    return pl.pallas_call(
        functools.partial(finish_body, rows),
        out_shape=(
            jax.ShapeDtypeStruct((3, rows, local), F32),
            jax.ShapeDtypeStruct((27, 2, local), F32),
        ),
        in_specs=[vmem()] * (3 + len(pieces)),
        out_specs=(vmem(),) * 2,
        compiler_params=PARAMS,
        name="finish",
    )(*near_core(query_sum, own_sum, tail_sum, *pieces))


def frame_pairs(step, flip):
    count = lax.axis_size("frames")
    return [(i, i ^ (2 * step + flip)) for i in range(count)]


def outer_pairs(direction):
    count = lax.axis_size("frames")
    moves = [(i, i + direction * (2 if i % 2 else -2)) for i in range(count)]
    return [(i, j) for i, j in moves if 0 <= j < count]


def exchange(block, pairs):
    return lax.ppermute(block, "frames", pairs)


def across(block):
    return lax.ppermute(block, "heads", [(0, 1), (1, 0)])


def scatter_weights(here, moved, rows):
    outer = lax.axis_size("frames") // 2
    summed = here + moved.astype(F32)
    end = outer * rows
    own = jnp.concatenate([summed[:rows], summed[end:]])
    low = summed.astype(BF16)
    pieces = []
    for step in range(1, outer):
        piece = jnp.concatenate([low[step * rows : (step + 1) * rows], low[end:]])
        pieces.append(exchange(piece, frame_pairs(step, 0)))
    return own, pieces


def add_all(own, pieces):
    for piece in pieces:
        own = own + piece.astype(F32)
    return own


def shards(tokens, out_grad, w_qkv, pool_kernel):
    local = tokens.shape[-1]
    heads_here = HEADS // lax.axis_size("heads")
    head_dim = local // heads_here
    rows, cols = tokens.shape[1], tokens.shape[2]
    token_count = rows * cols
    count = lax.axis_size("frames")
    frame = lax.axis_index("frames")
    core = lax.axis_index("heads")
    place = jnp.stack([frame, core]).astype(jnp.int32)
    outer = count // 2
    spare = round_up(local, LANES) - local
    own = jnp.pad(tokens.reshape(token_count, local), ((0, 0), (0, spare)))
    grad = out_grad.reshape(token_count, local)
    across_pair, barrier = frame_pairs(0, 1), lax.optimization_barrier
    other = across(own)
    grad_t = turn_call(grad, head_dim)
    other, grad_t = barrier((other, grad_t))
    weights = w_qkv.transpose(0, 2, 1)
    taps = pool_kernel.transpose(1, 0, 2)
    to_pair, to_next, inner, windows = pool_call(place, own, other, weights, taps, rows, cols)
    from_next = exchange(to_next, outer_pairs(1))
    from_pair = exchange(to_pair, across_pair)
    block = (inner + from_pair.astype(F32) + from_next.astype(F32)).astype(BF16)
    others = [exchange(block, frame_pairs(s, 0)) for s in range(1, outer)]
    other_first = exchange(block, across_pair)
    block, own, other = barrier((block, own, other))
    query_t, tokens_t = query_call(place, own, other, weights, head_dim)
    others, other_first, query_t, grad_t, tokens_t = barrier(
        (others, other_first, query_t, grad_t, tokens_t)
    )
    same_rest = jnp.concatenate(others)
    other_rest = exchange(same_rest, across_pair)
    sums, *saved = measure_call(block, same_rest, query_t, grad_t, head_dim)
    first_other, rest_other, *for_other, totals = attend_call(
        other_first, other_rest, query_t, grad_t, sums, head_dim
    )
    all_moved = exchange(jnp.concatenate([first_other, rest_other]), across_pair)
    step_rows = block.shape[0]
    first_same, rest_same, query_pad = attend_final_call(
        saved, query_t, grad_t, totals, for_other, head_dim, local, step_rows
    )
    first_moved, rest_moved = all_moved[:step_rows], all_moved[step_rows:]
    low = (rest_same.astype(F32) + rest_moved.astype(F32)).astype(BF16)
    pieces = [
        exchange(low[(s - 1) * step_rows : s * step_rows], frame_pairs(s, 0))
        for s in range(1, outer)
    ]
    query_back, query_here, query_away = query_side_call(
        place, query_pad, tokens_t, head_dim, count
    )
    query_moved = exchange(query_away, across_pair)
    pieces, first_moved, query_back, query_here = barrier(
        (pieces, first_moved, query_back, query_here)
    )
    summed = first_same.astype(F32) + first_moved.astype(F32)
    swapped = add_all(summed, pieces).astype(BF16)
    beside = exchange(swapped, outer_pairs(-1))
    mine = exchange(swapped, frame_pairs(0, 1))
    beside, mine = barrier((beside, mine))
    block_rows = 2 * local // count
    padded = round_up(block_rows, 8)
    here, away, backs = pull_call(
        place, mine, swapped, beside, windows, taps, tokens_t, rows, cols, count
    )
    query_moved, backs = barrier((query_moved, backs))
    near, far = token_call(place, query_back, backs, weights)
    moved = exchange(away, frame_pairs(0, 1))
    query_own, query_pieces = scatter_weights(query_here, query_moved, padded)
    moved, query_pieces = barrier((moved, query_pieces))
    query_sum = add_all(query_own, query_pieces)
    input_grad = (near + across(far)[:, :local].astype(F32)).astype(BF16)
    own_sum, pieces = scatter_weights(here, moved, padded)
    own_sum, tail_sum = own_sum[:padded], own_sum[padded:]
    pieces, input_grad, query_sum, own_sum, tail_sum = barrier(
        (pieces, input_grad, query_sum, own_sum, tail_sum)
    )
    weight_grad, kernel_grad = finish_call(
        query_sum, own_sum, tail_sum, pieces, block_rows, local
    )
    return input_grad.reshape(tokens.shape), weight_grad, kernel_grad.transpose(1, 0, 2)


def solution(mesh):
    in_specs = (
        P(("clips", "frames"), None, None, "heads"),
        P(("clips", "frames"), None, None, "heads"),
        P(None, None, "heads"),
        P(None, None, "heads"),
    )
    out_specs = (
        P(("clips", "frames"), None, None, "heads"),
        P("clips", "frames", "heads"),
        P("clips", None, "heads"),
    )
    return jax.shard_map(shards, mesh=mesh, in_specs=in_specs, out_specs=out_specs, check_vma=False)
```

```python
import functools
import math

import jax
import jax.numpy as jnp
from jax import lax
from jax.experimental import pallas as pl
from jax.experimental.pallas import tpu as pltpu
from jax.sharding import PartitionSpec as P

HEADS = 8
LANES = 128
STEP = 4
F32 = jnp.float32
BF16 = jnp.bfloat16
PARAMS = pltpu.CompilerParams(vmem_limit_bytes=24 * 1024 * 1024)
NN = (((1,), (0,)), ((), ()))
NT = (((1,), (1,)), ((), ()))
TN = (((0,), (0,)), ((), ()))


def mul(left, right, dims=NN):
    return lax.dot_general(left, right, dims, preferred_element_type=F32)


def near_core(*arrays):
    return tuple(pltpu.with_memory_space_constraint(x, pltpu.VMEM) for x in arrays)


def vmem():
    return pl.BlockSpec(memory_space=pltpu.VMEM)


def smem():
    return pl.BlockSpec(memory_space=pltpu.SMEM)


def lane_tiles(channels):
    return [
        (k, k * LANES, min(LANES, channels - k * LANES)) for k in range(pl.cdiv(channels, LANES))
    ]


def round_up(size, step):
    return pl.cdiv(size, step) * step


def join_taps(taps, joint):
    local = taps.shape[2]
    for side in range(2):
        joint[0:27, side * local : (side + 1) * local] = taps[:, side, :]


def pool_body(
    geometry, place, own, other, weights, taps, to_pair, to_next, inner, stored, windows, joint, wide
):
    rows, cols, local = geometry
    pooled_rows, pooled_cols = rows // 4, cols // 4
    even = place[0] % 2 == 0
    first = place[1] == 0
    mine, theirs = own[:, :local].astype(F32), other[:, :local].astype(F32)
    low_half = jnp.where(first, mine, theirs)
    high_half = jnp.where(first, theirs, mine)
    tokens = jnp.concatenate([low_half, high_half], axis=1).astype(BF16)
    join_taps(taps, joint)
    starts = lax.broadcasted_iota(jnp.int32, (pooled_cols, LANES), 0) == 0
    both = weights[1:3].reshape(2 * local, 2 * local)
    full = mul(tokens, both, NT).astype(BF16).astype(F32)
    for tile, low, width in lane_tiles(2 * local):
        wide[tile, 0:8, :] = jnp.zeros((8, LANES), F32)
        wide[tile, 8:, :width] = full[:, low : low + width]
        for b in range(3):
            for e in range(3):
                for i in range(pooled_rows):
                    row = 4 * i + b - 1
                    if row < 0:
                        piece = jnp.zeros((pooled_cols, LANES), F32)
                    else:
                        piece = wide[tile, pl.ds(row * cols + e + 7, pooled_cols, stride=4), :]
                        if e == 0:
                            piece = jnp.where(starts, 0.0, piece)
                    at = slice(i * pooled_cols, (i + 1) * pooled_cols)
                    windows[3 * b + e, at, low : low + width] = piece[:, :width]
    for k in range(9):
        stored[k] = windows[k].astype(BF16)
    sums = []
    for a in range(3):
        total = windows[0] * joint[9 * a : 9 * a + 1, :]
        for k in range(1, 9):
            total = total + windows[k] * joint[9 * a + k : 9 * a + k + 1, :]
        sums.append(total)
    earlier, center, later = sums
    to_pair[...] = center.astype(BF16)
    to_next[...] = jnp.where(even, later, earlier).astype(BF16)
    inner[...] = jnp.where(even, earlier, later)


def pool_call(place, own, other, weights, taps, rows, cols):
    both = weights.shape[2]
    count = rows * cols // 16
    return pl.pallas_call(
        functools.partial(pool_body, (rows, cols, both // 2)),
        out_shape=(
            pltpu.VMEM((count, both), BF16),
            pltpu.VMEM((count, both), BF16),
            pltpu.VMEM((count, both), F32),
            jax.ShapeDtypeStruct((9, count, both), BF16),
        ),
        in_specs=[smem()] + [vmem()] * 4,
        out_specs=(vmem(),) * 4,
        scratch_shapes=[
            pltpu.VMEM((9, count, both), F32),
            pltpu.VMEM((32, both), F32),
            pltpu.VMEM((pl.cdiv(both, LANES), rows * cols + 8, LANES), F32),
        ],
        compiler_params=PARAMS,
        name="project_pool",
    )(place, *near_core(own, other), weights, taps)


def spread_rows(head_dim, local, heads):
    rows = lax.broadcasted_iota(jnp.int32, (heads * LANES, local), 0)
    cols = lax.broadcasted_iota(jnp.int32, (heads * LANES, local), 1)
    chosen = rows < 0
    for h in range(heads):
        inside = (cols >= h * head_dim) & (cols < (h + 1) * head_dim)
        chosen = chosen | (inside & (rows == cols + h * (LANES - head_dim)))
    return chosen.astype(F32).astype(BF16)


def identity(size):
    rows = lax.broadcasted_iota(jnp.int32, (size, size), 0)
    cols = lax.broadcasted_iota(jnp.int32, (size, size), 1)
    return (rows == cols).astype(F32).astype(BF16)


def turn_body(geometry, out_grad, grad_t):
    head_dim, local, heads = geometry
    grad_t[...] = mul(spread_rows(head_dim, local, heads), out_grad[...], NT).astype(BF16)


def turn_call(out_grad, head_dim):
    tokens, local = out_grad.shape
    heads = local // head_dim
    return pl.pallas_call(
        functools.partial(turn_body, (head_dim, local, heads)),
        out_shape=pltpu.VMEM((heads * LANES, tokens), BF16),
        in_specs=[vmem()],
        out_specs=vmem(),
        compiler_params=PARAMS,
        name="turn_grad",
    )(out_grad)


def query_body(geometry, place, own, other, weights, query_t, tokens_t):
    head_dim, local, heads = geometry
    spread = spread_rows(head_dim, local, heads)
    turn = identity(local)
    near = pl.multiple_of(place[1] * local, 16)
    far = pl.multiple_of((1 - place[1]) * local, 16)
    tokens_t[pl.ds(near, local), :] = mul(turn, own[:, :local], NT).astype(BF16)
    tokens_t[pl.ds(far, local), :] = mul(turn, other[:, :local], NT).astype(BF16)
    query_t[...] = mul(mul(spread, weights[0]).astype(BF16), tokens_t[...]).astype(BF16)


def query_call(place, own, other, weights, head_dim):
    tokens, local = own.shape[0], weights.shape[1]
    heads = local // head_dim
    return pl.pallas_call(
        functools.partial(query_body, (head_dim, local, heads)),
        out_shape=(
            pltpu.VMEM((heads * LANES, tokens), BF16),
            pltpu.VMEM((2 * local, tokens), BF16),
        ),
        in_specs=[smem()] + [vmem()] * 3,
        out_specs=(vmem(),) * 2,
        compiler_params=PARAMS,
        name="project_query",
    )(place, *near_core(own, other), weights)


def choose_head(head_dim, local, head):
    rows = lax.broadcasted_iota(jnp.int32, (2 * local, 2 * LANES), 0)
    cols = lax.broadcasted_iota(jnp.int32, (2 * local, 2 * LANES), 1)
    lane = cols % LANES
    source = lane + (cols // LANES) * local + head * head_dim
    return ((rows == source) & (lane < head_dim)).astype(F32).astype(BF16)


def head_products(head_dim, keys, chosen, query, grad):
    both = jnp.concatenate([mul(part[...], chosen) for part in keys], axis=0).astype(BF16)
    key, value = both[:, :LANES], both[:, LANES:]
    factor = head_dim ** (-0.5) * math.log2(math.e)
    raised = jnp.exp2(mul(key, query) * factor)
    return key, raised, mul(value, grad)


def range_factor(total):
    return jnp.where(total > 1.0, 2.0**-16, 2.0**16)


def normalised(raised, total):
    factor = range_factor(total)
    return (raised * factor) * (1.0 / (jnp.maximum(total, 2.0**-125) * factor))


def measure_body(
    geometry, first, rest, query_t, grad_t, sums, share_out, prob_grad_out, key_pad
):
    head_dim, local, heads = geometry
    for sub in range(STEP):
        rows = slice(sub * LANES, (sub + 1) * LANES)
        chosen = choose_head(head_dim, local, STEP * pl.program_id(0) + sub)
        key, raised, prob_grad = head_products(
            head_dim, (first, rest), chosen, query_t[rows, :], grad_t[rows, :]
        )
        total = jnp.sum(raised, axis=0, keepdims=True)
        shares = normalised(raised, total)
        share_out[sub] = shares
        prob_grad_out[sub] = prob_grad
        key_pad[:, rows] = key
        sums[sub, 0:1, :] = total
        sums[sub, 1:2, :] = jnp.sum(shares * prob_grad, axis=0, keepdims=True)


def attend_body(geometry, final, *refs):
    head_dim, local, heads = geometry
    step = pl.program_id(0)
    scale = head_dim ** (-0.5)
    if final:
        own_shares, own_prob_grad, own_pad, query_t, grad_t, sums, *refs = refs
        other_pad, other_scores, first_grads, rest_grads, query_grad, total = refs
    else:
        first, rest, query_t, grad_t, sums, *refs = refs
        first_grads, rest_grads, key_pad, score_grads, totals, total = refs
    joined, choices = [], []
    for sub in range(STEP):
        rows = slice(sub * LANES, (sub + 1) * LANES)
        chosen = choose_head(head_dim, local, STEP * step + sub)
        query, grad = query_t[rows, :], grad_t[rows, :]
        if final:
            key, shares, prob_grad = own_pad[:, rows], own_shares[sub], own_prob_grad[sub]
            weight, centre = sums[sub, 0:1, :], sums[sub, 1:2, :]
        else:
            key, raised, prob_grad = head_products(head_dim, (first, rest), chosen, query, grad)
            first_sum, here_sum = sums[sub, 0:1, :], jnp.sum(raised, axis=0, keepdims=True)
            shares = normalised(raised, here_sum)
            whole = first_sum + here_sum
            factor = range_factor(whole)
            inverse = 1.0 / (whole * factor)
            first_weight, weight = first_sum * factor * inverse, here_sum * factor * inverse
            centre = sums[sub, 1:2, :] * first_weight + weight * jnp.sum(
                shares * prob_grad, axis=0, keepdims=True
            )
            totals[sub, 0:1, :] = first_weight
            totals[sub, 1:2, :] = centre
        probs = shares * weight
        score_grad = (probs * (prob_grad - centre) * scale).astype(BF16)
        if final:
            turn = identity(LANES)
            back_t = grad.astype(F32)
            for keys, scores in ((key, score_grad), (other_pad[:, rows], other_scores[sub])):
                back_t = back_t + mul(mul(turn, keys, NT).astype(BF16), scores)
            query_grad[:, rows] = back_t.T.astype(BF16)
        else:
            key_pad[:, rows] = key
            score_grads[sub] = score_grad
        value_back = mul(probs.astype(BF16), grad, NT)
        key_back = mul(score_grad, query, NT)
        joined += [key_back.astype(BF16), value_back.astype(BF16)]
        choices.append(chosen)
    placed = mul(jnp.concatenate(joined, axis=1), jnp.concatenate(choices, axis=1), NT)

    @pl.when(step == 0)
    def _():
        total[...] = placed

    @pl.when(step > 0)
    def _():
        total[...] += placed

    @pl.when(step == heads // STEP - 1)
    def _():
        split = first_grads.shape[0]
        first_grads[...] = total[:split, :].astype(BF16)
        rest_grads[...] = total[split:, :].astype(BF16)


def whole_spec(array):
    return pl.BlockSpec(array.shape, lambda h: (0,) * len(array.shape))


def head_specs(tokens, key_count):
    rows = pl.BlockSpec((STEP * LANES, tokens), lambda h: (h, 0))
    sums = pl.BlockSpec((STEP, 8, tokens), lambda h: (h, 0, 0))
    keys = pl.BlockSpec((key_count, STEP * LANES), lambda h: (0, h))
    scores = pl.BlockSpec((STEP, key_count, tokens), lambda h: (h, 0, 0))
    return rows, sums, keys, scores


def measure_call(first, rest, query_t, grad_t, head_dim):
    local, tokens = first.shape[1] // 2, query_t.shape[1]
    heads = local // head_dim
    key_count = first.shape[0] + rest.shape[0]
    row_spec, sum_spec, key_spec, score_spec = head_specs(tokens, key_count)
    return pl.pallas_call(
        functools.partial(measure_body, (head_dim, local, heads)),
        grid=(heads // STEP,),
        out_shape=(
            pltpu.VMEM((heads, 8, tokens), F32),
            pltpu.VMEM((heads, key_count, tokens), F32),
            pltpu.VMEM((heads, key_count, tokens), F32),
            pltpu.VMEM((key_count, heads * LANES), BF16),
        ),
        in_specs=[whole_spec(first), whole_spec(rest), row_spec, row_spec],
        out_specs=(sum_spec, score_spec, score_spec, key_spec),
        compiler_params=PARAMS,
        name="attend_measure",
    )(*near_core(first, rest, query_t, grad_t))


def attend_call(first, rest, query_t, grad_t, sums, head_dim):
    key_count, both = first.shape[0] + rest.shape[0], first.shape[1]
    local, tokens = both // 2, query_t.shape[1]
    heads = local // head_dim
    row_spec, sum_spec, key_spec, score_spec = head_specs(tokens, key_count)
    return pl.pallas_call(
        functools.partial(attend_body, (head_dim, local, heads), False),
        grid=(heads // STEP,),
        out_shape=(
            pltpu.VMEM(first.shape, BF16),
            pltpu.VMEM(rest.shape, BF16),
            pltpu.VMEM((key_count, heads * LANES), BF16),
            pltpu.VMEM((heads, key_count, tokens), BF16),
            pltpu.VMEM((heads, 8, tokens), F32),
        ),
        in_specs=[whole_spec(first), whole_spec(rest), row_spec, row_spec, sum_spec],
        out_specs=(whole_spec(first), whole_spec(rest), key_spec, score_spec, sum_spec),
        scratch_shapes=[pltpu.VMEM((key_count, both), F32)],
        compiler_params=PARAMS,
        name="attend_other",
    )(*near_core(first, rest, query_t, grad_t, sums))


def attend_final_call(saved, query_t, grad_t, totals, extra, head_dim, local, split):
    key_count, tokens = saved[0].shape[1:]
    heads = local // head_dim
    row_spec, sum_spec, key_spec, score_spec = head_specs(tokens, key_count)
    shapes = ((split, 2 * local), (key_count - split, 2 * local))
    outs = [pltpu.VMEM(shape, BF16) for shape in shapes]
    specs = [pl.BlockSpec(shape, lambda h: (0, 0)) for shape in shapes]
    in_specs = [score_spec, score_spec, key_spec, row_spec, row_spec, sum_spec]
    return pl.pallas_call(
        functools.partial(attend_body, (head_dim, local, heads), True),
        grid=(heads // STEP,),
        out_shape=(*outs, pltpu.VMEM((tokens, heads * LANES), BF16)),
        in_specs=[*in_specs, key_spec, score_spec],
        out_specs=(*specs, pl.BlockSpec((tokens, STEP * LANES), lambda h: (0, h))),
        scratch_shapes=[pltpu.VMEM((key_count, 2 * local), F32)],
        compiler_params=PARAMS,
        name="attend_same",
    )(*near_core(*saved, query_t, grad_t, totals, *extra))


def store_blocks(position, count, rows, column, here, away):
    padded = round_up(rows, 8)
    width = column.shape[1]
    for j in range(count):
        relative = position ^ j
        at = pl.multiple_of((relative // 2) * padded, 8)
        value = column[j * rows : (j + 1) * rows, :]

        @pl.when(relative % 2 == 0)
        def _(value=value, at=at):
            here[pl.ds(at, rows), :width] = value

        @pl.when(relative % 2 == 1)
        def _(value=value, at=at):
            away[pl.ds(at, rows), :width] = value.astype(BF16)


def query_side_body(geometry, place, query_pad, tokens_t, query_back, here, away):
    head_dim, local, heads, count = geometry
    spread = spread_rows(head_dim, local, heads)
    back = mul(query_pad[...], spread).astype(BF16)
    query_back[...] = back
    here[...] = jnp.zeros(here.shape, F32)
    away[...] = jnp.zeros(away.shape, BF16)
    column = mul(tokens_t[...], back)
    store_blocks(place[0], count, 2 * local // count, column, here, away)


def query_side_call(place, query_pad, tokens_t, head_dim, count):
    both, tokens = tokens_t.shape
    local = both // 2
    shape = (count // 2 * round_up(both // count, 8), round_up(local, LANES))
    return pl.pallas_call(
        functools.partial(query_side_body, (head_dim, local, local // head_dim, count)),
        out_shape=(
            pltpu.VMEM((tokens, local), BF16),
            pltpu.VMEM(shape, F32),
            pltpu.VMEM(shape, BF16),
        ),
        in_specs=[smem()] + [vmem()] * 2,
        out_specs=(vmem(),) * 3,
        compiler_params=PARAMS,
        name="query_side",
    )(place, *near_core(query_pad, tokens_t))


def pull_body(
    geometry,
    place,
    mine,
    swapped,
    beside,
    windows,
    taps,
    tokens_t,
    here,
    away,
    backs,
    wide,
    staged,
    joint,
    folded,
):
    rows, cols, local, count = geometry
    pooled_rows, pooled_cols = rows // 4, cols // 4
    position = place[0]
    even = position % 2 == 0
    pooled = pooled_rows * pooled_cols
    block_rows = 2 * local // count
    padded = round_up(block_rows, 8)
    outer = count // 2
    join_taps(taps, joint)
    starts = lax.broadcasted_iota(jnp.int32, (pooled, 2 * local), 0) % pooled_cols == 0
    folded[...] = jnp.zeros(folded.shape, F32)
    wide[...] = jnp.zeros(wide.shape, F32)
    if padded > block_rows:
        here[...] = jnp.zeros(here.shape, F32)
        away[...] = jnp.zeros(away.shape, BF16)
    partner, distant = swapped[...].astype(F32), beside[...].astype(F32)
    grads = [
        jnp.where(even, partner, distant),
        mine[...].astype(F32),
        jnp.where(even, distant, partner),
    ]
    for b in range(3):
        for e in range(3):
            k = 3 * b + e
            window = windows[k].astype(F32)
            spread = None
            for a in range(3):
                term = grads[a] * joint[9 * a + k : 9 * a + k + 1, :]
                spread = term if spread is None else spread + term
                folded[9 * a + k : 9 * a + k + 1, :] = jnp.sum(
                    grads[a] * window, axis=0, keepdims=True
                )
            if e == 0:
                spread = jnp.where(starts, 0.0, spread)
            for tile, low, width in lane_tiles(2 * local):
                staged[tile, :, :width] = spread[:, low : low + width]
                for i in range(pooled_rows):
                    row = 4 * i + b - 1
                    if row >= 0:
                        at = slice(i * pooled_cols, (i + 1) * pooled_cols)
                        wide[tile, pl.ds(row * cols + e + 7, pooled_cols, stride=4), :] = staged[
                            tile, at, :
                        ]
    back = jnp.concatenate(
        [wide[tile, 8:, :width] for tile, low, width in lane_tiles(2 * local)], axis=1
    ).astype(BF16)
    backs[...] = back
    column = mul(tokens_t[...], back)
    here[outer * padded :, :] = folded[...]
    away[outer * padded :, :] = folded[...].astype(BF16)
    store_blocks(position, count, block_rows, column, here, away)


def token_body(place, query_back, backs, weights, token_near, token_far):
    local = weights.shape[1]
    both = weights[1:3].reshape(2 * local, 2 * local)
    token_sum = mul(query_back[...], weights[0]) + mul(backs[...], both)
    first = place[1] == 0
    low_half, high_half = token_sum[:, :local], token_sum[:, local:]
    token_near[...] = jnp.where(first, low_half, high_half)
    token_far[:, :local] = jnp.where(first, high_half, low_half).astype(BF16)
    token_far[:, local:] = jnp.zeros((token_far.shape[0], token_far.shape[1] - local), BF16)


def token_call(place, query_back, backs, weights):
    tokens, local = query_back.shape
    return pl.pallas_call(
        token_body,
        out_shape=(
            pltpu.VMEM((tokens, local), F32),
            pltpu.VMEM((tokens, round_up(local, LANES)), BF16),
        ),
        in_specs=[smem()] + [vmem()] * 3,
        out_specs=(vmem(),) * 2,
        compiler_params=PARAMS,
        name="token_side",
    )(place, *near_core(query_back, backs), weights)


def pull_call(
    place, mine, swapped, beside, windows, taps, tokens_t, rows, cols, count
):
    both, tokens = tokens_t.shape
    local = both // 2
    padded = round_up(both // count, 8)
    size = count // 2 * padded + 32
    tiles = pl.cdiv(both, LANES)
    return pl.pallas_call(
        functools.partial(pull_body, (rows, cols, local, count)),
        out_shape=(
            pltpu.VMEM((size, both), F32),
            pltpu.VMEM((size, both), BF16),
            pltpu.VMEM((tokens, both), BF16),
        ),
        in_specs=[smem()] + [vmem()] * 6,
        out_specs=(vmem(),) * 3,
        scratch_shapes=[
            pltpu.VMEM((tiles, tokens + 8, LANES), F32),
            pltpu.VMEM((tiles, rows * cols // 16, LANES), F32),
            pltpu.VMEM((32, both), F32),
            pltpu.VMEM((32, both), F32),
        ],
        compiler_params=PARAMS,
        name="pull_back",
    )(
        place,
        *near_core(mine, swapped, beside),
        windows,
        taps,
        *near_core(tokens_t),
    )


def finish_body(rows, query_sum, own_sum, tail_sum, *refs):
    *pieces, weight_grad, kernel_grad = refs
    local = weight_grad.shape[2]
    padded = own_sum.shape[0]
    total, tail = own_sum[...], tail_sum[...]
    for piece in pieces:
        total = total + piece[:padded, :].astype(F32)
        tail = tail + piece[padded:, :].astype(F32)
    weight_grad[0] = query_sum[:rows, :local]
    weight_grad[1] = total[:rows, :local]
    weight_grad[2] = total[:rows, local:]
    for side in range(2):
        for k in range(kernel_grad.shape[0]):
            kernel_grad[k, side : side + 1, :] = tail[k : k + 1, side * local : (side + 1) * local]


def finish_call(query_sum, own_sum, tail_sum, pieces, rows, local):
    return pl.pallas_call(
        functools.partial(finish_body, rows),
        out_shape=(
            jax.ShapeDtypeStruct((3, rows, local), F32),
            jax.ShapeDtypeStruct((27, 2, local), F32),
        ),
        in_specs=[vmem()] * (3 + len(pieces)),
        out_specs=(vmem(),) * 2,
        compiler_params=PARAMS,
        name="finish",
    )(*near_core(query_sum, own_sum, tail_sum, *pieces))


def frame_pairs(step, flip):
    count = lax.axis_size("frames")
    return [(i, i ^ (2 * step + flip)) for i in range(count)]


def outer_pairs(direction):
    count = lax.axis_size("frames")
    moves = [(i, i + direction * (2 if i % 2 else -2)) for i in range(count)]
    return [(i, j) for i, j in moves if 0 <= j < count]


def exchange(block, pairs):
    return lax.ppermute(block, "frames", pairs)


def across(block):
    return lax.ppermute(block, "heads", [(0, 1), (1, 0)])


def scatter_weights(here, moved, rows):
    outer = lax.axis_size("frames") // 2
    summed = here + moved.astype(F32)
    end = outer * rows
    own = jnp.concatenate([summed[:rows], summed[end:]])
    low = summed.astype(BF16)
    pieces = []
    for step in range(1, outer):
        piece = jnp.concatenate([low[step * rows : (step + 1) * rows], low[end:]])
        pieces.append(exchange(piece, frame_pairs(step, 0)))
    return own, pieces


def add_all(own, pieces):
    for piece in pieces:
        own = own + piece.astype(F32)
    return own


def shards(tokens, out_grad, w_qkv, pool_kernel):
    local = tokens.shape[-1]
    heads_here = HEADS // lax.axis_size("heads")
    head_dim = local // heads_here
    rows, cols = tokens.shape[1], tokens.shape[2]
    token_count = rows * cols
    count = lax.axis_size("frames")
    frame = lax.axis_index("frames")
    core = lax.axis_index("heads")
    place = jnp.stack([frame, core]).astype(jnp.int32)
    outer = count // 2
    spare = round_up(local, LANES) - local
    own = jnp.pad(tokens.reshape(token_count, local), ((0, 0), (0, spare)))
    grad = out_grad.reshape(token_count, local)
    across_pair, barrier = frame_pairs(0, 1), lax.optimization_barrier
    other = across(own)
    grad_t = turn_call(grad, head_dim)
    other, grad_t = barrier((other, grad_t))
    weights = w_qkv.transpose(0, 2, 1)
    taps = pool_kernel.transpose(1, 0, 2)
    to_pair, to_next, inner, windows = pool_call(place, own, other, weights, taps, rows, cols)
    from_next = exchange(to_next, outer_pairs(1))
    from_pair = exchange(to_pair, across_pair)
    block = (inner + from_pair.astype(F32) + from_next.astype(F32)).astype(BF16)
    others = [exchange(block, frame_pairs(s, 0)) for s in range(1, outer)]
    other_first = exchange(block, across_pair)
    block, own, other = barrier((block, own, other))
    query_t, tokens_t = query_call(place, own, other, weights, head_dim)
    others, other_first, query_t, grad_t, tokens_t = barrier(
        (others, other_first, query_t, grad_t, tokens_t)
    )
    same_rest = jnp.concatenate(others)
    other_rest = exchange(same_rest, across_pair)
    sums, *saved = measure_call(block, same_rest, query_t, grad_t, head_dim)
    first_other, rest_other, *for_other, totals = attend_call(
        other_first, other_rest, query_t, grad_t, sums, head_dim
    )
    all_moved = exchange(jnp.concatenate([first_other, rest_other]), across_pair)
    step_rows = block.shape[0]
    first_same, rest_same, query_pad = attend_final_call(
        saved, query_t, grad_t, totals, for_other, head_dim, local, step_rows
    )
    first_moved, rest_moved = all_moved[:step_rows], all_moved[step_rows:]
    low = (rest_same.astype(F32) + rest_moved.astype(F32)).astype(BF16)
    pieces = [
        exchange(low[(s - 1) * step_rows : s * step_rows], frame_pairs(s, 0))
        for s in range(1, outer)
    ]
    query_back, query_here, query_away = query_side_call(
        place, query_pad, tokens_t, head_dim, count
    )
    query_moved = exchange(query_away, across_pair)
    pieces, first_moved, query_back, query_here = barrier(
        (pieces, first_moved, query_back, query_here)
    )
    summed = first_same.astype(F32) + first_moved.astype(F32)
    swapped = add_all(summed, pieces).astype(BF16)
    beside = exchange(swapped, outer_pairs(-1))
    mine = exchange(swapped, frame_pairs(0, 1))
    beside, mine = barrier((beside, mine))
    block_rows = 2 * local // count
    padded = round_up(block_rows, 8)
    here, away, backs = pull_call(
        place, mine, swapped, beside, windows, taps, tokens_t, rows, cols, count
    )
    query_moved, backs = barrier((query_moved, backs))
    near, far = token_call(place, query_back, backs, weights)
    moved = exchange(away, frame_pairs(0, 1))
    query_own, query_pieces = scatter_weights(query_here, query_moved, padded)
    moved, query_pieces = barrier((moved, query_pieces))
    query_sum = add_all(query_own, query_pieces)
    input_grad = (near + across(far)[:, :local].astype(F32)).astype(BF16)
    own_sum, pieces = scatter_weights(here, moved, padded)
    own_sum, tail_sum = own_sum[:padded], own_sum[padded:]
    pieces, input_grad, query_sum, own_sum, tail_sum = barrier(
        (pieces, input_grad, query_sum, own_sum, tail_sum)
    )
    weight_grad, kernel_grad = finish_call(
        query_sum, own_sum, tail_sum, pieces, block_rows, local
    )
    return input_grad.reshape(tokens.shape), weight_grad, kernel_grad.transpose(1, 0, 2)


def solution(mesh):
    in_specs = (
        P(("clips", "frames"), None, None, "heads"),
        P(("clips", "frames"), None, None, "heads"),
        P(None, None, "heads"),
        P(None, None, "heads"),
    )
    out_specs = (
        P(("clips", "frames"), None, None, "heads"),
        P("clips", "frames", "heads"),
        P("clips", None, "heads"),
    )
    return jax.shard_map(shards, mesh=mesh, in_specs=in_specs, out_specs=out_specs, check_vma=False)
```

```python
import functools
import math

import jax
import jax.numpy as jnp
from jax import lax
from jax.experimental import pallas as pl
from jax.experimental.pallas import tpu as pltpu
from jax.sharding import PartitionSpec as P

HEADS = 8
LANES = 128
STEP = 4
F32 = jnp.float32
BF16 = jnp.bfloat16
PARAMS = pltpu.CompilerParams(vmem_limit_bytes=24 * 1024 * 1024)
NN = (((1,), (0,)), ((), ()))
NT = (((1,), (1,)), ((), ()))
TN = (((0,), (0,)), ((), ()))


def mul(left, right, dims=NN):
    return lax.dot_general(left, right, dims, preferred_element_type=F32)


def near_core(*arrays):
    return tuple(pltpu.with_memory_space_constraint(x, pltpu.VMEM) for x in arrays)


def vmem():
    return pl.BlockSpec(memory_space=pltpu.VMEM)


def smem():
    return pl.BlockSpec(memory_space=pltpu.SMEM)


def lane_tiles(channels):
    return [
        (k, k * LANES, min(LANES, channels - k * LANES)) for k in range(pl.cdiv(channels, LANES))
    ]


def round_up(size, step):
    return pl.cdiv(size, step) * step


def join_taps(taps, joint):
    local = taps.shape[2]
    for side in range(2):
        joint[0:27, side * local : (side + 1) * local] = taps[:, side, :]


def pool_body(
    geometry, place, own, other, weights, taps, to_pair, to_next, inner, stored, windows, joint, wide
):
    rows, cols, local = geometry
    pooled_rows, pooled_cols = rows // 4, cols // 4
    even = place[0] % 2 == 0
    first = place[1] == 0
    mine, theirs = own[:, :local].astype(F32), other[:, :local].astype(F32)
    low_half = jnp.where(first, mine, theirs)
    high_half = jnp.where(first, theirs, mine)
    tokens = jnp.concatenate([low_half, high_half], axis=1).astype(BF16)
    join_taps(taps, joint)
    starts = lax.broadcasted_iota(jnp.int32, (pooled_cols, LANES), 0) == 0
    both = weights[1:3].reshape(2 * local, 2 * local)
    full = mul(tokens, both, NT).astype(BF16).astype(F32)
    for tile, low, width in lane_tiles(2 * local):
        wide[tile, 0:8, :] = jnp.zeros((8, LANES), F32)
        wide[tile, 8:, :width] = full[:, low : low + width]
        for b in range(3):
            for e in range(3):
                for i in range(pooled_rows):
                    row = 4 * i + b - 1
                    if row < 0:
                        piece = jnp.zeros((pooled_cols, LANES), F32)
                    else:
                        piece = wide[tile, pl.ds(row * cols + e + 7, pooled_cols, stride=4), :]
                        if e == 0:
                            piece = jnp.where(starts, 0.0, piece)
                    at = slice(i * pooled_cols, (i + 1) * pooled_cols)
                    windows[3 * b + e, at, low : low + width] = piece[:, :width]
    for k in range(9):
        stored[k] = windows[k].astype(BF16)
    sums = []
    for a in range(3):
        total = windows[0] * joint[9 * a : 9 * a + 1, :]
        for k in range(1, 9):
            total = total + windows[k] * joint[9 * a + k : 9 * a + k + 1, :]
        sums.append(total)
    earlier, center, later = sums
    to_pair[...] = center.astype(BF16)
    to_next[...] = jnp.where(even, later, earlier).astype(BF16)
    inner[...] = jnp.where(even, earlier, later)


def pool_call(place, own, other, weights, taps, rows, cols):
    both = weights.shape[2]
    count = rows * cols // 16
    return pl.pallas_call(
        functools.partial(pool_body, (rows, cols, both // 2)),
        out_shape=(
            pltpu.VMEM((count, both), BF16),
            pltpu.VMEM((count, both), BF16),
            pltpu.VMEM((count, both), F32),
            jax.ShapeDtypeStruct((9, count, both), BF16),
        ),
        in_specs=[smem()] + [vmem()] * 4,
        out_specs=(vmem(),) * 4,
        scratch_shapes=[
            pltpu.VMEM((9, count, both), F32),
            pltpu.VMEM((32, both), F32),
            pltpu.VMEM((pl.cdiv(both, LANES), rows * cols + 8, LANES), F32),
        ],
        compiler_params=PARAMS,
        name="project_pool",
    )(place, *near_core(own, other), weights, taps)


def spread_rows(head_dim, local, heads):
    rows = lax.broadcasted_iota(jnp.int32, (heads * LANES, local), 0)
    cols = lax.broadcasted_iota(jnp.int32, (heads * LANES, local), 1)
    chosen = rows < 0
    for h in range(heads):
        inside = (cols >= h * head_dim) & (cols < (h + 1) * head_dim)
        chosen = chosen | (inside & (rows == cols + h * (LANES - head_dim)))
    return chosen.astype(F32).astype(BF16)


def identity(size):
    rows = lax.broadcasted_iota(jnp.int32, (size, size), 0)
    cols = lax.broadcasted_iota(jnp.int32, (size, size), 1)
    return (rows == cols).astype(F32).astype(BF16)


def turn_body(geometry, out_grad, grad_t):
    head_dim, local, heads = geometry
    grad_t[...] = mul(spread_rows(head_dim, local, heads), out_grad[...], NT).astype(BF16)


def turn_call(out_grad, head_dim):
    tokens, local = out_grad.shape
    heads = local // head_dim
    return pl.pallas_call(
        functools.partial(turn_body, (head_dim, local, heads)),
        out_shape=pltpu.VMEM((heads * LANES, tokens), BF16),
        in_specs=[vmem()],
        out_specs=vmem(),
        compiler_params=PARAMS,
        name="turn_grad",
    )(out_grad)


def query_body(geometry, place, own, other, weights, query_t, tokens_t):
    head_dim, local, heads = geometry
    spread = spread_rows(head_dim, local, heads)
    turn = identity(local)
    near = pl.multiple_of(place[1] * local, 16)
    far = pl.multiple_of((1 - place[1]) * local, 16)
    tokens_t[pl.ds(near, local), :] = mul(turn, own[:, :local], NT).astype(BF16)
    tokens_t[pl.ds(far, local), :] = mul(turn, other[:, :local], NT).astype(BF16)
    query_t[...] = mul(mul(spread, weights[0]).astype(BF16), tokens_t[...]).astype(BF16)


def query_call(place, own, other, weights, head_dim):
    tokens, local = own.shape[0], weights.shape[1]
    heads = local // head_dim
    return pl.pallas_call(
        functools.partial(query_body, (head_dim, local, heads)),
        out_shape=(
            pltpu.VMEM((heads * LANES, tokens), BF16),
            pltpu.VMEM((2 * local, tokens), BF16),
        ),
        in_specs=[smem()] + [vmem()] * 3,
        out_specs=(vmem(),) * 2,
        compiler_params=PARAMS,
        name="project_query",
    )(place, *near_core(own, other), weights)


def choose_head(head_dim, local, head):
    rows = lax.broadcasted_iota(jnp.int32, (2 * local, 2 * LANES), 0)
    cols = lax.broadcasted_iota(jnp.int32, (2 * local, 2 * LANES), 1)
    lane = cols % LANES
    source = lane + (cols // LANES) * local + head * head_dim
    return ((rows == source) & (lane < head_dim)).astype(F32).astype(BF16)


def head_products(head_dim, keys, chosen, query, grad):
    both = jnp.concatenate([mul(part[...], chosen) for part in keys], axis=0).astype(BF16)
    key, value = both[:, :LANES], both[:, LANES:]
    factor = head_dim ** (-0.5) * math.log2(math.e)
    raised = jnp.exp2(mul(key, query) * factor)
    return key, raised, mul(value, grad)


def range_factor(total):
    return jnp.where(total > 1.0, 2.0**-16, 2.0**16)


def normalised(raised, total):
    factor = range_factor(total)
    return (raised * factor) * (1.0 / (jnp.maximum(total, 2.0**-125) * factor))


def measure_body(
    geometry, first, rest, query_t, grad_t, sums, share_out, prob_grad_out, key_pad
):
    head_dim, local, heads = geometry
    for sub in range(STEP):
        rows = slice(sub * LANES, (sub + 1) * LANES)
        chosen = choose_head(head_dim, local, STEP * pl.program_id(0) + sub)
        key, raised, prob_grad = head_products(
            head_dim, (first, rest), chosen, query_t[rows, :], grad_t[rows, :]
        )
        total = jnp.sum(raised, axis=0, keepdims=True)
        shares = normalised(raised, total)
        share_out[sub] = shares
        prob_grad_out[sub] = prob_grad
        key_pad[:, rows] = key
        sums[sub, 0:1, :] = total
        sums[sub, 1:2, :] = jnp.sum(shares * prob_grad, axis=0, keepdims=True)


def attend_body(geometry, final, *refs):
    head_dim, local, heads = geometry
    step = pl.program_id(0)
    scale = head_dim ** (-0.5)
    if final:
        own_shares, own_prob_grad, own_pad, query_t, grad_t, sums, *refs = refs
        other_pad, other_scores, key_grads, query_grad, total = refs
    else:
        first, rest, query_t, grad_t, sums, *refs = refs
        key_grads, key_pad, score_grads, totals, total = refs
    joined, choices = [], []
    for sub in range(STEP):
        rows = slice(sub * LANES, (sub + 1) * LANES)
        chosen = choose_head(head_dim, local, STEP * step + sub)
        query, grad = query_t[rows, :], grad_t[rows, :]
        if final:
            key, shares, prob_grad = own_pad[:, rows], own_shares[sub], own_prob_grad[sub]
            weight, centre = sums[sub, 0:1, :], sums[sub, 1:2, :]
        else:
            key, raised, prob_grad = head_products(head_dim, (first, rest), chosen, query, grad)
            first_sum, here_sum = sums[sub, 0:1, :], jnp.sum(raised, axis=0, keepdims=True)
            shares = normalised(raised, here_sum)
            whole = first_sum + here_sum
            factor = range_factor(whole)
            inverse = 1.0 / (whole * factor)
            first_weight, weight = first_sum * factor * inverse, here_sum * factor * inverse
            centre = sums[sub, 1:2, :] * first_weight + weight * jnp.sum(
                shares * prob_grad, axis=0, keepdims=True
            )
            totals[sub, 0:1, :] = first_weight
            totals[sub, 1:2, :] = centre
        probs = shares * weight
        score_grad = (probs * (prob_grad - centre) * scale).astype(BF16)
        if final:
            turn = identity(LANES)
            back_t = grad.astype(F32)
            for keys, scores in ((key, score_grad), (other_pad[:, rows], other_scores[sub])):
                back_t = back_t + mul(mul(turn, keys, NT).astype(BF16), scores)
            query_grad[:, rows] = back_t.T.astype(BF16)
        else:
            key_pad[:, rows] = key
            score_grads[sub] = score_grad
        value_back = mul(probs.astype(BF16), grad, NT)
        key_back = mul(score_grad, query, NT)
        joined += [key_back.astype(BF16), value_back.astype(BF16)]
        choices.append(chosen)
    placed = mul(jnp.concatenate(joined, axis=1), jnp.concatenate(choices, axis=1), NT)

    @pl.when(step == 0)
    def _():
        total[...] = placed

    @pl.when(step > 0)
    def _():
        total[...] += placed

    @pl.when(step == heads // STEP - 1)
    def _():
        key_grads[...] = total[...].astype(BF16)


def whole_spec(array):
    return pl.BlockSpec(array.shape, lambda h: (0,) * len(array.shape))


def head_specs(tokens, key_count):
    rows = pl.BlockSpec((STEP * LANES, tokens), lambda h: (h, 0))
    sums = pl.BlockSpec((STEP, 8, tokens), lambda h: (h, 0, 0))
    keys = pl.BlockSpec((key_count, STEP * LANES), lambda h: (0, h))
    scores = pl.BlockSpec((STEP, key_count, tokens), lambda h: (h, 0, 0))
    return rows, sums, keys, scores


def measure_call(first, rest, query_t, grad_t, head_dim):
    local, tokens = first.shape[1] // 2, query_t.shape[1]
    heads = local // head_dim
    key_count = first.shape[0] + rest.shape[0]
    row_spec, sum_spec, key_spec, score_spec = head_specs(tokens, key_count)
    return pl.pallas_call(
        functools.partial(measure_body, (head_dim, local, heads)),
        grid=(heads // STEP,),
        out_shape=(
            pltpu.VMEM((heads, 8, tokens), F32),
            pltpu.VMEM((heads, key_count, tokens), F32),
            pltpu.VMEM((heads, key_count, tokens), F32),
            pltpu.VMEM((key_count, heads * LANES), BF16),
        ),
        in_specs=[whole_spec(first), whole_spec(rest), row_spec, row_spec],
        out_specs=(sum_spec, score_spec, score_spec, key_spec),
        compiler_params=PARAMS,
        name="attend_measure",
    )(*near_core(first, rest, query_t, grad_t))


def attend_call(first, rest, query_t, grad_t, sums, head_dim):
    key_count, both = first.shape[0] + rest.shape[0], first.shape[1]
    local, tokens = both // 2, query_t.shape[1]
    heads = local // head_dim
    row_spec, sum_spec, key_spec, score_spec = head_specs(tokens, key_count)
    return pl.pallas_call(
        functools.partial(attend_body, (head_dim, local, heads), False),
        grid=(heads // STEP,),
        out_shape=(
            pltpu.VMEM((key_count, both), BF16),
            pltpu.VMEM((key_count, heads * LANES), BF16),
            pltpu.VMEM((heads, key_count, tokens), BF16),
            pltpu.VMEM((heads, 8, tokens), F32),
        ),
        in_specs=[whole_spec(first), whole_spec(rest), row_spec, row_spec, sum_spec],
        out_specs=(
            pl.BlockSpec((key_count, both), lambda h: (0, 0)),
            key_spec,
            score_spec,
            sum_spec,
        ),
        scratch_shapes=[pltpu.VMEM((key_count, both), F32)],
        compiler_params=PARAMS,
        name="attend_other",
    )(*near_core(first, rest, query_t, grad_t, sums))


def attend_final_call(saved, query_t, grad_t, totals, extra, head_dim, local):
    key_count, tokens = saved[0].shape[1:]
    heads = local // head_dim
    row_spec, sum_spec, key_spec, score_spec = head_specs(tokens, key_count)
    shape = (key_count, 2 * local)
    outs = [pltpu.VMEM(shape, BF16)]
    specs = [pl.BlockSpec(shape, lambda h: (0, 0))]
    in_specs = [score_spec, score_spec, key_spec, row_spec, row_spec, sum_spec]
    return pl.pallas_call(
        functools.partial(attend_body, (head_dim, local, heads), True),
        grid=(heads // STEP,),
        out_shape=(*outs, pltpu.VMEM((tokens, heads * LANES), BF16)),
        in_specs=[*in_specs, key_spec, score_spec],
        out_specs=(*specs, pl.BlockSpec((tokens, STEP * LANES), lambda h: (0, h))),
        scratch_shapes=[pltpu.VMEM((key_count, 2 * local), F32)],
        compiler_params=PARAMS,
        name="attend_same",
    )(*near_core(*saved, query_t, grad_t, totals, *extra))


def store_blocks(position, count, rows, column, here, away):
    padded = round_up(rows, 8)
    width = column.shape[1]
    for j in range(count):
        relative = position ^ j
        at = pl.multiple_of((relative // 2) * padded, 8)
        value = column[j * rows : (j + 1) * rows, :]

        @pl.when(relative % 2 == 0)
        def _(value=value, at=at):
            here[pl.ds(at, rows), :width] = value

        @pl.when(relative % 2 == 1)
        def _(value=value, at=at):
            away[pl.ds(at, rows), :width] = value.astype(BF16)


def query_side_body(geometry, place, query_pad, tokens_t, query_back, here, away):
    head_dim, local, heads, count = geometry
    spread = spread_rows(head_dim, local, heads)
    back = mul(query_pad[...], spread).astype(BF16)
    query_back[...] = back
    here[...] = jnp.zeros(here.shape, F32)
    away[...] = jnp.zeros(away.shape, BF16)
    column = mul(tokens_t[...], back)
    store_blocks(place[0], count, 2 * local // count, column, here, away)


def query_side_call(place, query_pad, tokens_t, head_dim, count):
    both, tokens = tokens_t.shape
    local = both // 2
    shape = (count // 2 * round_up(both // count, 8), round_up(local, LANES))
    return pl.pallas_call(
        functools.partial(query_side_body, (head_dim, local, local // head_dim, count)),
        out_shape=(
            pltpu.VMEM((tokens, local), BF16),
            pltpu.VMEM(shape, F32),
            pltpu.VMEM(shape, BF16),
        ),
        in_specs=[smem()] + [vmem()] * 2,
        out_specs=(vmem(),) * 3,
        compiler_params=PARAMS,
        name="query_side",
    )(place, *near_core(query_pad, tokens_t))


def tap_packing(both, padded):
    spare = round_up(both, LANES) - both
    fits = spare > 0 and both % spare == 0 and padded >= 8 * (both // spare)
    return spare, 8 if fits else 0


def pull_body(
    geometry,
    place,
    mine,
    swapped,
    beside,
    windows,
    taps,
    tokens_t,
    here,
    away,
    backs,
    wide,
    staged,
    joint,
    folded,
):
    rows, cols, local, count = geometry
    pooled_rows, pooled_cols = rows // 4, cols // 4
    position = place[0]
    even = position % 2 == 0
    pooled = pooled_rows * pooled_cols
    block_rows = 2 * local // count
    padded = round_up(block_rows, 8)
    outer = count // 2
    join_taps(taps, joint)
    starts = lax.broadcasted_iota(jnp.int32, (pooled, 2 * local), 0) % pooled_cols == 0
    folded[...] = jnp.zeros(folded.shape, F32)
    wide[...] = jnp.zeros(wide.shape, F32)
    if padded > block_rows:
        here[...] = jnp.zeros(here.shape, F32)
        away[...] = jnp.zeros(away.shape, BF16)
    partner, distant = swapped[...].astype(F32), beside[...].astype(F32)
    grads = [
        jnp.where(even, partner, distant),
        mine[...].astype(F32),
        jnp.where(even, distant, partner),
    ]
    for b in range(3):
        for e in range(3):
            k = 3 * b + e
            window = windows[k].astype(F32)
            spread = None
            for a in range(3):
                term = grads[a] * joint[9 * a + k : 9 * a + k + 1, :]
                spread = term if spread is None else spread + term
                folded[9 * a + k : 9 * a + k + 1, :] = jnp.sum(
                    grads[a] * window, axis=0, keepdims=True
                )
            if e == 0:
                spread = jnp.where(starts, 0.0, spread)
            for tile, low, width in lane_tiles(2 * local):
                staged[tile, :, :width] = spread[:, low : low + width]
                for i in range(pooled_rows):
                    row = 4 * i + b - 1
                    if row >= 0:
                        at = slice(i * pooled_cols, (i + 1) * pooled_cols)
                        wide[tile, pl.ds(row * cols + e + 7, pooled_cols, stride=4), :] = staged[
                            tile, at, :
                        ]
    back = jnp.concatenate(
        [wide[tile, 8:, :width] for tile, low, width in lane_tiles(2 * local)], axis=1
    ).astype(BF16)
    backs[...] = back
    column = mul(tokens_t[...], back)
    both, end = 2 * local, outer * padded
    spare, packed = tap_packing(both, padded)
    tail = here.shape[0] - end
    for target in (here, away):
        if spare > 0:
            target[:, both:] = jnp.zeros((target.shape[0], spare), target.dtype)
        target[end:, :both] = folded[packed : packed + tail, :].astype(target.dtype)
        for g in range(both // spare if packed else 0):
            part = folded[0:8, g * spare : (g + 1) * spare].astype(target.dtype)
            for s in range(outer):
                at = s * padded + 8 * g
                target[at : at + 8, both:] = part
    store_blocks(position, count, block_rows, column, here, away)


def token_body(place, query_back, backs, weights, token_near, token_far):
    local = weights.shape[1]
    both = weights[1:3].reshape(2 * local, 2 * local)
    token_sum = mul(query_back[...], weights[0]) + mul(backs[...], both)
    first = place[1] == 0
    low_half, high_half = token_sum[:, :local], token_sum[:, local:]
    token_near[...] = jnp.where(first, low_half, high_half)
    token_far[:, :local] = jnp.where(first, high_half, low_half).astype(BF16)
    token_far[:, local:] = jnp.zeros((token_far.shape[0], token_far.shape[1] - local), BF16)


def token_call(place, query_back, backs, weights):
    tokens, local = query_back.shape
    return pl.pallas_call(
        token_body,
        out_shape=(
            pltpu.VMEM((tokens, local), F32),
            pltpu.VMEM((tokens, round_up(local, LANES)), BF16),
        ),
        in_specs=[smem()] + [vmem()] * 3,
        out_specs=(vmem(),) * 2,
        compiler_params=PARAMS,
        name="token_side",
    )(place, *near_core(query_back, backs), weights)


def pull_call(
    place, mine, swapped, beside, windows, taps, tokens_t, rows, cols, count
):
    both, tokens = tokens_t.shape
    local = both // 2
    padded = round_up(both // count, 8)
    spare, packed = tap_packing(both, padded)
    size = count // 2 * padded + 32 - packed
    tiles = pl.cdiv(both, LANES)
    return pl.pallas_call(
        functools.partial(pull_body, (rows, cols, local, count)),
        out_shape=(
            pltpu.VMEM((size, both + spare), F32),
            pltpu.VMEM((size, both + spare), BF16),
            pltpu.VMEM((tokens, both), BF16),
        ),
        in_specs=[smem()] + [vmem()] * 6,
        out_specs=(vmem(),) * 3,
        scratch_shapes=[
            pltpu.VMEM((tiles, tokens + 8, LANES), F32),
            pltpu.VMEM((tiles, rows * cols // 16, LANES), F32),
            pltpu.VMEM((32, both), F32),
            pltpu.VMEM((32, both), F32),
        ],
        compiler_params=PARAMS,
        name="pull_back",
    )(
        place,
        *near_core(mine, swapped, beside),
        windows,
        taps,
        *near_core(tokens_t),
    )


def finish_body(rows, query_sum, own_sum, tail_sum, *refs):
    *pieces, weight_grad, kernel_grad = refs
    local = weight_grad.shape[2]
    padded = own_sum.shape[0]
    total, tail = own_sum[...], tail_sum[...]
    for piece in pieces:
        total = total + piece[:padded, :].astype(F32)
        tail = tail + piece[padded:, :].astype(F32)
    weight_grad[0] = query_sum[:rows, :local]
    weight_grad[1] = total[:rows, :local]
    weight_grad[2] = total[:rows, local : 2 * local]
    both = 2 * local
    spare, packed = tap_packing(both, padded)
    tail = tail[:, :both]
    if packed:
        parts = [total[8 * g : 8 * g + 8, both:] for g in range(both // spare)]
        tail = jnp.concatenate([jnp.concatenate(parts, axis=1), tail], axis=0)
    for side in range(2):
        for k in range(kernel_grad.shape[0]):
            kernel_grad[k, side : side + 1, :] = tail[k : k + 1, side * local : (side + 1) * local]


def finish_call(query_sum, own_sum, tail_sum, pieces, rows, local):
    return pl.pallas_call(
        functools.partial(finish_body, rows),
        out_shape=(
            jax.ShapeDtypeStruct((3, rows, local), F32),
            jax.ShapeDtypeStruct((27, 2, local), F32),
        ),
        in_specs=[vmem()] * (3 + len(pieces)),
        out_specs=(vmem(),) * 2,
        compiler_params=PARAMS,
        name="finish",
    )(*near_core(query_sum, own_sum, tail_sum, *pieces))


def frame_pairs(step, flip):
    count = lax.axis_size("frames")
    return [(i, i ^ (2 * step + flip)) for i in range(count)]


def outer_pairs(direction):
    count = lax.axis_size("frames")
    moves = [(i, i + direction * (2 if i % 2 else -2)) for i in range(count)]
    return [(i, j) for i, j in moves if 0 <= j < count]


def exchange(block, pairs):
    return lax.ppermute(block, "frames", pairs)


def across(block):
    return lax.ppermute(block, "heads", [(0, 1), (1, 0)])


def scatter_weights(here, moved, rows):
    outer = lax.axis_size("frames") // 2
    summed = here + moved.astype(F32)
    end = outer * rows
    own = jnp.concatenate([summed[:rows], summed[end:]])
    low = summed.astype(BF16)
    pieces = []
    for step in range(1, outer):
        piece = jnp.concatenate([low[step * rows : (step + 1) * rows], low[end:]])
        pieces.append(exchange(piece, frame_pairs(step, 0)))
    return own, pieces


def add_all(own, pieces):
    for piece in pieces:
        own = own + piece.astype(F32)
    return own


def shards(tokens, out_grad, w_qkv, pool_kernel):
    local = tokens.shape[-1]
    heads_here = HEADS // lax.axis_size("heads")
    head_dim = local // heads_here
    rows, cols = tokens.shape[1], tokens.shape[2]
    token_count = rows * cols
    count = lax.axis_size("frames")
    frame = lax.axis_index("frames")
    core = lax.axis_index("heads")
    place = jnp.stack([frame, core]).astype(jnp.int32)
    outer = count // 2
    spare = round_up(local, LANES) - local
    own = jnp.pad(tokens.reshape(token_count, local), ((0, 0), (0, spare)))
    grad = out_grad.reshape(token_count, local)
    across_pair, barrier = frame_pairs(0, 1), lax.optimization_barrier
    other = across(own)
    grad_t = turn_call(grad, head_dim)
    other, grad_t = barrier((other, grad_t))
    weights = w_qkv.transpose(0, 2, 1)
    taps = pool_kernel.transpose(1, 0, 2)
    to_pair, to_next, inner, windows = pool_call(place, own, other, weights, taps, rows, cols)
    from_next = exchange(to_next, outer_pairs(1))
    from_pair = exchange(to_pair, across_pair)
    block = (inner + from_pair.astype(F32) + from_next.astype(F32)).astype(BF16)
    others = [exchange(block, frame_pairs(s, 0)) for s in range(1, outer)]
    other_first = exchange(block, across_pair)
    block, own, other = barrier((block, own, other))
    query_t, tokens_t = query_call(place, own, other, weights, head_dim)
    others, other_first, query_t, grad_t, tokens_t = barrier(
        (others, other_first, query_t, grad_t, tokens_t)
    )
    same_rest = jnp.concatenate(others)
    other_rest = exchange(same_rest, across_pair)
    sums, *saved = measure_call(block, same_rest, query_t, grad_t, head_dim)
    other_grads, *for_other, totals = attend_call(
        other_first, other_rest, query_t, grad_t, sums, head_dim
    )
    all_moved = exchange(other_grads, across_pair)
    step_rows = block.shape[0]
    same_grads, query_pad = attend_final_call(
        saved, query_t, grad_t, totals, for_other, head_dim, local
    )
    all_sum = same_grads.astype(F32) + all_moved.astype(F32)
    low = all_sum[step_rows:].astype(BF16)
    pieces = [
        exchange(low[(s - 1) * step_rows : s * step_rows], frame_pairs(s, 0))
        for s in range(1, outer)
    ]
    query_back, query_here, query_away = query_side_call(
        place, query_pad, tokens_t, head_dim, count
    )
    query_moved = exchange(query_away, across_pair)
    pieces, query_back, query_here = barrier((pieces, query_back, query_here))
    swapped = add_all(all_sum[:step_rows], pieces).astype(BF16)
    beside = exchange(swapped, outer_pairs(-1))
    mine = exchange(swapped, frame_pairs(0, 1))
    beside, mine = barrier((beside, mine))
    block_rows = 2 * local // count
    padded = round_up(block_rows, 8)
    here, away, backs = pull_call(
        place, mine, swapped, beside, windows, taps, tokens_t, rows, cols, count
    )
    query_moved, backs = barrier((query_moved, backs))
    near, far = token_call(place, query_back, backs, weights)
    moved = exchange(away, frame_pairs(0, 1))
    query_own, query_pieces = scatter_weights(query_here, query_moved, padded)
    moved, query_pieces = barrier((moved, query_pieces))
    query_sum = add_all(query_own, query_pieces)
    input_grad = (near + across(far)[:, :local].astype(F32)).astype(BF16)
    own_sum, pieces = scatter_weights(here, moved, padded)
    own_sum, tail_sum = own_sum[:padded], own_sum[padded:]
    pieces, input_grad, query_sum, own_sum, tail_sum = barrier(
        (pieces, input_grad, query_sum, own_sum, tail_sum)
    )
    weight_grad, kernel_grad = finish_call(
        query_sum, own_sum, tail_sum, pieces, block_rows, local
    )
    return input_grad.reshape(tokens.shape), weight_grad, kernel_grad.transpose(1, 0, 2)


def solution(mesh):
    in_specs = (
        P(("clips", "frames"), None, None, "heads"),
        P(("clips", "frames"), None, None, "heads"),
        P(None, None, "heads"),
        P(None, None, "heads"),
    )
    out_specs = (
        P(("clips", "frames"), None, None, "heads"),
        P("clips", "frames", "heads"),
        P("clips", None, "heads"),
    )
    return jax.shard_map(shards, mesh=mesh, in_specs=in_specs, out_specs=out_specs, check_vma=False)
```

```python
import functools
import math

import jax
import jax.numpy as jnp
from jax import lax
from jax.experimental import pallas as pl
from jax.experimental.pallas import tpu as pltpu
from jax.sharding import PartitionSpec as P

HEADS = 8
LANES = 128
STEP = 4
F32 = jnp.float32
BF16 = jnp.bfloat16
PARAMS = pltpu.CompilerParams(vmem_limit_bytes=24 * 1024 * 1024)
NN = (((1,), (0,)), ((), ()))
NT = (((1,), (1,)), ((), ()))
TN = (((0,), (0,)), ((), ()))


def mul(left, right, dims=NN):
    return lax.dot_general(left, right, dims, preferred_element_type=F32)


def near_core(*arrays):
    return tuple(pltpu.with_memory_space_constraint(x, pltpu.VMEM) for x in arrays)


def vmem():
    return pl.BlockSpec(memory_space=pltpu.VMEM)


def smem():
    return pl.BlockSpec(memory_space=pltpu.SMEM)


def lane_tiles(channels):
    return [
        (k, k * LANES, min(LANES, channels - k * LANES)) for k in range(pl.cdiv(channels, LANES))
    ]


def round_up(size, step):
    return pl.cdiv(size, step) * step


def join_taps(taps, joint):
    local = taps.shape[2]
    for side in range(2):
        joint[0:27, side * local : (side + 1) * local] = taps[:, side, :]


def pool_body(
    geometry, place, own, other, weights, taps, to_pair, to_next, inner, stored, windows, joint, wide
):
    rows, cols, local = geometry
    pooled_rows, pooled_cols = rows // 4, cols // 4
    even = place[0] % 2 == 0
    first = place[1] == 0
    mine, theirs = own[:, :local].astype(F32), other[:, :local].astype(F32)
    low_half = jnp.where(first, mine, theirs)
    high_half = jnp.where(first, theirs, mine)
    tokens = jnp.concatenate([low_half, high_half], axis=1).astype(BF16)
    join_taps(taps, joint)
    starts = lax.broadcasted_iota(jnp.int32, (pooled_cols, LANES), 0) == 0
    both = weights[1:3].reshape(2 * local, 2 * local)
    full = mul(tokens, both, NT).astype(BF16).astype(F32)
    for tile, low, width in lane_tiles(2 * local):
        wide[tile, 0:8, :] = jnp.zeros((8, LANES), F32)
        wide[tile, 8:, :width] = full[:, low : low + width]
        for b in range(3):
            for e in range(3):
                for i in range(pooled_rows):
                    row = 4 * i + b - 1
                    if row < 0:
                        piece = jnp.zeros((pooled_cols, LANES), F32)
                    else:
                        piece = wide[tile, pl.ds(row * cols + e + 7, pooled_cols, stride=4), :]
                        if e == 0:
                            piece = jnp.where(starts, 0.0, piece)
                    at = slice(i * pooled_cols, (i + 1) * pooled_cols)
                    windows[3 * b + e, at, low : low + width] = piece[:, :width]
    for k in range(9):
        stored[k] = windows[k].astype(BF16)
    sums = []
    for a in range(3):
        total = windows[0] * joint[9 * a : 9 * a + 1, :]
        for k in range(1, 9):
            total = total + windows[k] * joint[9 * a + k : 9 * a + k + 1, :]
        sums.append(total)
    earlier, center, later = sums
    to_pair[...] = center.astype(BF16)
    to_next[...] = jnp.where(even, later, earlier).astype(BF16)
    inner[...] = jnp.where(even, earlier, later)


def pool_call(place, own, other, weights, taps, rows, cols):
    both = weights.shape[2]
    count = rows * cols // 16
    return pl.pallas_call(
        functools.partial(pool_body, (rows, cols, both // 2)),
        out_shape=(
            pltpu.VMEM((count, both), BF16),
            pltpu.VMEM((count, both), BF16),
            pltpu.VMEM((count, both), F32),
            jax.ShapeDtypeStruct((9, count, both), BF16),
        ),
        in_specs=[smem()] + [vmem()] * 4,
        out_specs=(vmem(),) * 4,
        scratch_shapes=[
            pltpu.VMEM((9, count, both), F32),
            pltpu.VMEM((32, both), F32),
            pltpu.VMEM((pl.cdiv(both, LANES), rows * cols + 8, LANES), F32),
        ],
        compiler_params=PARAMS,
        name="project_pool",
    )(place, *near_core(own, other), weights, taps)


def spread_rows(head_dim, local, heads):
    rows = lax.broadcasted_iota(jnp.int32, (heads * LANES, local), 0)
    cols = lax.broadcasted_iota(jnp.int32, (heads * LANES, local), 1)
    chosen = rows < 0
    for h in range(heads):
        inside = (cols >= h * head_dim) & (cols < (h + 1) * head_dim)
        chosen = chosen | (inside & (rows == cols + h * (LANES - head_dim)))
    return chosen.astype(F32).astype(BF16)


def identity(size):
    rows = lax.broadcasted_iota(jnp.int32, (size, size), 0)
    cols = lax.broadcasted_iota(jnp.int32, (size, size), 1)
    return (rows == cols).astype(F32).astype(BF16)


def turn_body(geometry, out_grad, grad_t):
    head_dim, local, heads = geometry
    grad_t[...] = mul(spread_rows(head_dim, local, heads), out_grad[...], NT).astype(BF16)


def turn_call(out_grad, head_dim):
    tokens, local = out_grad.shape
    heads = local // head_dim
    return pl.pallas_call(
        functools.partial(turn_body, (head_dim, local, heads)),
        out_shape=pltpu.VMEM((heads * LANES, tokens), BF16),
        in_specs=[vmem()],
        out_specs=vmem(),
        compiler_params=PARAMS,
        name="turn_grad",
    )(out_grad)


def query_body(geometry, place, own, other, weights, query_t, tokens_t):
    head_dim, local, heads = geometry
    spread = spread_rows(head_dim, local, heads)
    turn = identity(local)
    near = pl.multiple_of(place[1] * local, 16)
    far = pl.multiple_of((1 - place[1]) * local, 16)
    tokens_t[pl.ds(near, local), :] = mul(turn, own[:, :local], NT).astype(BF16)
    tokens_t[pl.ds(far, local), :] = mul(turn, other[:, :local], NT).astype(BF16)
    query_t[...] = mul(mul(spread, weights[0]).astype(BF16), tokens_t[...]).astype(BF16)


def query_call(place, own, other, weights, head_dim):
    tokens, local = own.shape[0], weights.shape[1]
    heads = local // head_dim
    return pl.pallas_call(
        functools.partial(query_body, (head_dim, local, heads)),
        out_shape=(
            pltpu.VMEM((heads * LANES, tokens), BF16),
            pltpu.VMEM((2 * local, tokens), BF16),
        ),
        in_specs=[smem()] + [vmem()] * 3,
        out_specs=(vmem(),) * 2,
        compiler_params=PARAMS,
        name="project_query",
    )(place, *near_core(own, other), weights)


def choose_head(head_dim, local, head):
    rows = lax.broadcasted_iota(jnp.int32, (2 * local, 2 * LANES), 0)
    cols = lax.broadcasted_iota(jnp.int32, (2 * local, 2 * LANES), 1)
    lane = cols % LANES
    source = lane + (cols // LANES) * local + head * head_dim
    return ((rows == source) & (lane < head_dim)).astype(F32).astype(BF16)


def head_products(head_dim, keys, chosen, query, grad):
    both = jnp.concatenate([mul(part[...], chosen) for part in keys], axis=0).astype(BF16)
    key, value = both[:, :LANES], both[:, LANES:]
    factor = head_dim ** (-0.5) * math.log2(math.e)
    raised = jnp.exp2(mul(key, query) * factor)
    return key, raised, mul(value, grad)


def range_factor(total):
    return jnp.where(total > 1.0, 2.0**-16, 2.0**16)


def normalised(raised, total):
    factor = range_factor(total)
    return (raised * factor) * (1.0 / (jnp.maximum(total, 2.0**-125) * factor))


def measure_body(
    geometry, first, rest, query_t, grad_t, sums, share_out, prob_grad_out, key_pad
):
    head_dim, local, heads = geometry
    for sub in range(STEP):
        rows = slice(sub * LANES, (sub + 1) * LANES)
        chosen = choose_head(head_dim, local, STEP * pl.program_id(0) + sub)
        key, raised, prob_grad = head_products(
            head_dim, (first, rest), chosen, query_t[rows, :], grad_t[rows, :]
        )
        total = jnp.sum(raised, axis=0, keepdims=True)
        shares = normalised(raised, total)
        share_out[sub] = shares
        prob_grad_out[sub] = prob_grad
        key_pad[:, rows] = key
        sums[sub, 0:1, :] = total
        sums[sub, 1:2, :] = jnp.sum(shares * prob_grad, axis=0, keepdims=True)


def attend_body(geometry, final, *refs):
    head_dim, local, heads = geometry
    step = pl.program_id(0)
    scale = head_dim ** (-0.5)
    if final:
        own_shares, own_prob_grad, own_pad, query_t, grad_t, sums, *refs = refs
        other_pad, other_scores, key_grads, query_grad, total = refs
    else:
        first, rest, query_t, grad_t, sums, *refs = refs
        key_grads, key_pad, score_grads, totals, total = refs
    joined, choices = [], []
    for sub in range(STEP):
        rows = slice(sub * LANES, (sub + 1) * LANES)
        chosen = choose_head(head_dim, local, STEP * step + sub)
        query, grad = query_t[rows, :], grad_t[rows, :]
        if final:
            key, shares, prob_grad = own_pad[:, rows], own_shares[sub], own_prob_grad[sub]
            weight, centre = sums[sub, 0:1, :], sums[sub, 1:2, :]
        else:
            key, raised, prob_grad = head_products(head_dim, (first, rest), chosen, query, grad)
            first_sum, here_sum = sums[sub, 0:1, :], jnp.sum(raised, axis=0, keepdims=True)
            shares = normalised(raised, here_sum)
            whole = first_sum + here_sum
            factor = range_factor(whole)
            inverse = 1.0 / (whole * factor)
            first_weight, weight = first_sum * factor * inverse, here_sum * factor * inverse
            centre = sums[sub, 1:2, :] * first_weight + weight * jnp.sum(
                shares * prob_grad, axis=0, keepdims=True
            )
            totals[sub, 0:1, :] = first_weight
            totals[sub, 1:2, :] = centre
        probs = shares * weight
        score_grad = (probs * (prob_grad - centre) * scale).astype(BF16)
        if final:
            turn = identity(LANES)
            back_t = grad.astype(F32)
            for keys, scores in ((key, score_grad), (other_pad[:, rows], other_scores[sub])):
                back_t = back_t + mul(mul(turn, keys, NT).astype(BF16), scores)
            query_grad[:, rows] = back_t.T.astype(BF16)
        else:
            key_pad[:, rows] = key
            score_grads[sub] = score_grad
        value_back = mul(probs.astype(BF16), grad, NT)
        key_back = mul(score_grad, query, NT)
        joined += [key_back.astype(BF16), value_back.astype(BF16)]
        choices.append(chosen)
    placed = mul(jnp.concatenate(joined, axis=1), jnp.concatenate(choices, axis=1), NT)

    @pl.when(step == 0)
    def _():
        total[...] = placed

    @pl.when(step > 0)
    def _():
        total[...] += placed

    @pl.when(step == heads // STEP - 1)
    def _():
        key_grads[...] = total[...].astype(BF16)


def whole_spec(array):
    return pl.BlockSpec(array.shape, lambda h: (0,) * len(array.shape))


def head_specs(tokens, key_count):
    rows = pl.BlockSpec((STEP * LANES, tokens), lambda h: (h, 0))
    sums = pl.BlockSpec((STEP, 8, tokens), lambda h: (h, 0, 0))
    keys = pl.BlockSpec((key_count, STEP * LANES), lambda h: (0, h))
    scores = pl.BlockSpec((STEP, key_count, tokens), lambda h: (h, 0, 0))
    return rows, sums, keys, scores


def measure_call(first, rest, query_t, grad_t, head_dim):
    local, tokens = first.shape[1] // 2, query_t.shape[1]
    heads = local // head_dim
    key_count = first.shape[0] + rest.shape[0]
    row_spec, sum_spec, key_spec, score_spec = head_specs(tokens, key_count)
    return pl.pallas_call(
        functools.partial(measure_body, (head_dim, local, heads)),
        grid=(heads // STEP,),
        out_shape=(
            pltpu.VMEM((heads, 8, tokens), F32),
            pltpu.VMEM((heads, key_count, tokens), F32),
            pltpu.VMEM((heads, key_count, tokens), F32),
            pltpu.VMEM((key_count, heads * LANES), BF16),
        ),
        in_specs=[whole_spec(first), whole_spec(rest), row_spec, row_spec],
        out_specs=(sum_spec, score_spec, score_spec, key_spec),
        compiler_params=PARAMS,
        name="attend_measure",
    )(*near_core(first, rest, query_t, grad_t))


def attend_call(first, rest, query_t, grad_t, sums, head_dim):
    key_count, both = first.shape[0] + rest.shape[0], first.shape[1]
    local, tokens = both // 2, query_t.shape[1]
    heads = local // head_dim
    row_spec, sum_spec, key_spec, score_spec = head_specs(tokens, key_count)
    return pl.pallas_call(
        functools.partial(attend_body, (head_dim, local, heads), False),
        grid=(heads // STEP,),
        out_shape=(
            pltpu.VMEM((key_count, both), BF16),
            pltpu.VMEM((key_count, heads * LANES), BF16),
            pltpu.VMEM((heads, key_count, tokens), BF16),
            pltpu.VMEM((heads, 8, tokens), F32),
        ),
        in_specs=[whole_spec(first), whole_spec(rest), row_spec, row_spec, sum_spec],
        out_specs=(
            pl.BlockSpec((key_count, both), lambda h: (0, 0)),
            key_spec,
            score_spec,
            sum_spec,
        ),
        scratch_shapes=[pltpu.VMEM((key_count, both), F32)],
        compiler_params=PARAMS,
        name="attend_other",
    )(*near_core(first, rest, query_t, grad_t, sums))


def attend_final_call(saved, query_t, grad_t, totals, extra, head_dim, local):
    key_count, tokens = saved[0].shape[1:]
    heads = local // head_dim
    row_spec, sum_spec, key_spec, score_spec = head_specs(tokens, key_count)
    shape = (key_count, 2 * local)
    outs = [pltpu.VMEM(shape, BF16)]
    specs = [pl.BlockSpec(shape, lambda h: (0, 0))]
    in_specs = [score_spec, score_spec, key_spec, row_spec, row_spec, sum_spec]
    return pl.pallas_call(
        functools.partial(attend_body, (head_dim, local, heads), True),
        grid=(heads // STEP,),
        out_shape=(*outs, pltpu.VMEM((tokens, heads * LANES), BF16)),
        in_specs=[*in_specs, key_spec, score_spec],
        out_specs=(*specs, pl.BlockSpec((tokens, STEP * LANES), lambda h: (0, h))),
        scratch_shapes=[pltpu.VMEM((key_count, 2 * local), F32)],
        compiler_params=PARAMS,
        name="attend_same",
    )(*near_core(*saved, query_t, grad_t, totals, *extra))


def store_blocks(position, count, rows, column, here, away):
    padded = round_up(rows, 8)
    width = column.shape[1]
    for j in range(count):
        relative = position ^ j
        at = pl.multiple_of((relative // 2) * padded, 8)
        value = column[j * rows : (j + 1) * rows, :]

        @pl.when(relative % 2 == 0)
        def _(value=value, at=at):
            here[pl.ds(at, rows), :width] = value

        @pl.when(relative % 2 == 1)
        def _(value=value, at=at):
            away[pl.ds(at, rows), :width] = value.astype(BF16)


def query_side_body(geometry, place, query_pad, tokens_t, query_back, here, away):
    head_dim, local, heads, count = geometry
    spread = spread_rows(head_dim, local, heads)
    back = mul(query_pad[...], spread).astype(BF16)
    query_back[...] = back
    here[...] = jnp.zeros(here.shape, F32)
    away[...] = jnp.zeros(away.shape, BF16)
    column = mul(tokens_t[...], back)
    store_blocks(place[0], count, 2 * local // count, column, here, away)


def query_side_call(place, query_pad, tokens_t, head_dim, count):
    both, tokens = tokens_t.shape
    local = both // 2
    shape = (count // 2 * round_up(both // count, 8), round_up(local, LANES))
    return pl.pallas_call(
        functools.partial(query_side_body, (head_dim, local, local // head_dim, count)),
        out_shape=(
            pltpu.VMEM((tokens, local), BF16),
            pltpu.VMEM(shape, F32),
            pltpu.VMEM(shape, BF16),
        ),
        in_specs=[smem()] + [vmem()] * 2,
        out_specs=(vmem(),) * 3,
        compiler_params=PARAMS,
        name="query_side",
    )(place, *near_core(query_pad, tokens_t))


def tap_packing(both, padded):
    spare = round_up(both, LANES) - both
    fits = spare > 0 and both % spare == 0 and padded >= 8 * (both // spare)
    return spare, 8 if fits else 0


def pull_body(
    geometry,
    place,
    mine,
    swapped,
    beside,
    windows,
    taps,
    tokens_t,
    here,
    away,
    backs,
    wide,
    staged,
    joint,
    folded,
):
    rows, cols, local, count = geometry
    pooled_rows, pooled_cols = rows // 4, cols // 4
    position = place[0]
    even = position % 2 == 0
    pooled = pooled_rows * pooled_cols
    block_rows = 2 * local // count
    padded = round_up(block_rows, 8)
    outer = count // 2
    join_taps(taps, joint)
    starts = lax.broadcasted_iota(jnp.int32, (pooled, 2 * local), 0) % pooled_cols == 0
    folded[...] = jnp.zeros(folded.shape, F32)
    wide[...] = jnp.zeros(wide.shape, F32)
    if padded > block_rows:
        here[...] = jnp.zeros(here.shape, F32)
        away[...] = jnp.zeros(away.shape, BF16)
    partner, distant = swapped[...].astype(F32), beside[...].astype(F32)
    grads = [
        jnp.where(even, partner, distant),
        mine[...].astype(F32),
        jnp.where(even, distant, partner),
    ]
    for b in range(3):
        for e in range(3):
            k = 3 * b + e
            window = windows[k].astype(F32)
            spread = None
            for a in range(3):
                term = grads[a] * joint[9 * a + k : 9 * a + k + 1, :]
                spread = term if spread is None else spread + term
                folded[9 * a + k : 9 * a + k + 1, :] = jnp.sum(
                    grads[a] * window, axis=0, keepdims=True
                )
            if e == 0:
                spread = jnp.where(starts, 0.0, spread)
            for tile, low, width in lane_tiles(2 * local):
                staged[tile, :, :width] = spread[:, low : low + width]
                for i in range(pooled_rows):
                    row = 4 * i + b - 1
                    if row >= 0:
                        at = slice(i * pooled_cols, (i + 1) * pooled_cols)
                        wide[tile, pl.ds(row * cols + e + 7, pooled_cols, stride=4), :] = staged[
                            tile, at, :
                        ]
    back = jnp.concatenate(
        [wide[tile, 8:, :width] for tile, low, width in lane_tiles(2 * local)], axis=1
    ).astype(BF16)
    backs[...] = back
    column = mul(tokens_t[...], back)
    both, end = 2 * local, outer * padded
    spare, packed = tap_packing(both, padded)
    tail = here.shape[0] - end
    for target in (here, away):
        if spare > 0:
            target[:, both:] = jnp.zeros((target.shape[0], spare), target.dtype)
        target[end:, :both] = folded[packed : packed + tail, :].astype(target.dtype)
        for g in range(both // spare if packed else 0):
            part = folded[0:8, g * spare : (g + 1) * spare].astype(target.dtype)
            for s in range(outer):
                at = s * padded + 8 * g
                target[at : at + 8, both:] = part
    store_blocks(position, count, block_rows, column, here, away)


def token_body(place, query_back, backs, weights, token_near, token_far):
    local = weights.shape[1]
    joined = jnp.concatenate([query_back[...], backs[...]], axis=1)
    token_sum = mul(joined, weights[...].reshape(3 * local, 2 * local))
    first = place[1] == 0
    low_half, high_half = token_sum[:, :local], token_sum[:, local:]
    token_near[...] = jnp.where(first, low_half, high_half)
    token_far[:, :local] = jnp.where(first, high_half, low_half).astype(BF16)
    token_far[:, local:] = jnp.zeros((token_far.shape[0], token_far.shape[1] - local), BF16)


def token_call(place, query_back, backs, weights):
    tokens, local = query_back.shape
    return pl.pallas_call(
        token_body,
        out_shape=(
            pltpu.VMEM((tokens, local), F32),
            pltpu.VMEM((tokens, round_up(local, LANES)), BF16),
        ),
        in_specs=[smem()] + [vmem()] * 3,
        out_specs=(vmem(),) * 2,
        compiler_params=PARAMS,
        name="token_side",
    )(place, *near_core(query_back, backs), weights)


def pull_call(
    place, mine, swapped, beside, windows, taps, tokens_t, rows, cols, count
):
    both, tokens = tokens_t.shape
    local = both // 2
    padded = round_up(both // count, 8)
    spare, packed = tap_packing(both, padded)
    size = count // 2 * padded + 32 - packed
    tiles = pl.cdiv(both, LANES)
    return pl.pallas_call(
        functools.partial(pull_body, (rows, cols, local, count)),
        out_shape=(
            pltpu.VMEM((size, both + spare), F32),
            pltpu.VMEM((size, both + spare), BF16),
            pltpu.VMEM((tokens, both), BF16),
        ),
        in_specs=[smem()] + [vmem()] * 6,
        out_specs=(vmem(),) * 3,
        scratch_shapes=[
            pltpu.VMEM((tiles, tokens + 8, LANES), F32),
            pltpu.VMEM((tiles, rows * cols // 16, LANES), F32),
            pltpu.VMEM((32, both), F32),
            pltpu.VMEM((32, both), F32),
        ],
        compiler_params=PARAMS,
        name="pull_back",
    )(
        place,
        *near_core(mine, swapped, beside),
        windows,
        taps,
        *near_core(tokens_t),
    )


def finish_body(rows, query_sum, own_sum, tail_sum, *refs):
    *pieces, weight_grad, kernel_grad = refs
    local = weight_grad.shape[2]
    padded = own_sum.shape[0]
    total, tail = own_sum[...], tail_sum[...]
    for piece in pieces:
        total = total + piece[:padded, :].astype(F32)
        tail = tail + piece[padded:, :].astype(F32)
    weight_grad[0] = query_sum[:rows, :local]
    weight_grad[1] = total[:rows, :local]
    weight_grad[2] = total[:rows, local : 2 * local]
    both = 2 * local
    spare, packed = tap_packing(both, padded)
    tail = tail[:, :both]
    if packed:
        parts = [total[8 * g : 8 * g + 8, both:] for g in range(both // spare)]
        tail = jnp.concatenate([jnp.concatenate(parts, axis=1), tail], axis=0)
    for side in range(2):
        for k in range(kernel_grad.shape[0]):
            kernel_grad[k, side : side + 1, :] = tail[k : k + 1, side * local : (side + 1) * local]


def finish_call(query_sum, own_sum, tail_sum, pieces, rows, local):
    return pl.pallas_call(
        functools.partial(finish_body, rows),
        out_shape=(
            jax.ShapeDtypeStruct((3, rows, local), F32),
            jax.ShapeDtypeStruct((27, 2, local), F32),
        ),
        in_specs=[vmem()] * (3 + len(pieces)),
        out_specs=(vmem(),) * 2,
        compiler_params=PARAMS,
        name="finish",
    )(*near_core(query_sum, own_sum, tail_sum, *pieces))


def frame_pairs(step, flip):
    count = lax.axis_size("frames")
    return [(i, i ^ (2 * step + flip)) for i in range(count)]


def outer_pairs(direction):
    count = lax.axis_size("frames")
    moves = [(i, i + direction * (2 if i % 2 else -2)) for i in range(count)]
    return [(i, j) for i, j in moves if 0 <= j < count]


def exchange(block, pairs):
    return lax.ppermute(block, "frames", pairs)


def across(block):
    return lax.ppermute(block, "heads", [(0, 1), (1, 0)])


def scatter_weights(here, moved, rows):
    outer = lax.axis_size("frames") // 2
    summed = here + moved.astype(F32)
    end = outer * rows
    own = jnp.concatenate([summed[:rows], summed[end:]])
    low = summed.astype(BF16)
    pieces = []
    for step in range(1, outer):
        piece = jnp.concatenate([low[step * rows : (step + 1) * rows], low[end:]])
        pieces.append(exchange(piece, frame_pairs(step, 0)))
    return own, pieces


def add_all(own, pieces):
    for piece in pieces:
        own = own + piece.astype(F32)
    return own


def shards(tokens, out_grad, w_qkv, pool_kernel):
    local = tokens.shape[-1]
    heads_here = HEADS // lax.axis_size("heads")
    head_dim = local // heads_here
    rows, cols = tokens.shape[1], tokens.shape[2]
    token_count = rows * cols
    count = lax.axis_size("frames")
    frame = lax.axis_index("frames")
    core = lax.axis_index("heads")
    place = jnp.stack([frame, core]).astype(jnp.int32)
    outer = count // 2
    spare = round_up(local, LANES) - local
    own = jnp.pad(tokens.reshape(token_count, local), ((0, 0), (0, spare)))
    grad = out_grad.reshape(token_count, local)
    across_pair, barrier = frame_pairs(0, 1), lax.optimization_barrier
    other = across(own)
    grad_t = turn_call(grad, head_dim)
    other, grad_t = barrier((other, grad_t))
    weights = w_qkv.transpose(0, 2, 1)
    taps = pool_kernel.transpose(1, 0, 2)
    to_pair, to_next, inner, windows = pool_call(place, own, other, weights, taps, rows, cols)
    from_next = exchange(to_next, outer_pairs(1))
    from_pair = exchange(to_pair, across_pair)
    block = (inner + from_pair.astype(F32) + from_next.astype(F32)).astype(BF16)
    others = [exchange(block, frame_pairs(s, 0)) for s in range(1, outer)]
    other_first = exchange(block, across_pair)
    block, own, other = barrier((block, own, other))
    query_t, tokens_t = query_call(place, own, other, weights, head_dim)
    others, other_first, query_t, grad_t, tokens_t = barrier(
        (others, other_first, query_t, grad_t, tokens_t)
    )
    same_rest = jnp.concatenate(others)
    other_rest = exchange(same_rest, across_pair)
    sums, *saved = measure_call(block, same_rest, query_t, grad_t, head_dim)
    other_grads, *for_other, totals = attend_call(
        other_first, other_rest, query_t, grad_t, sums, head_dim
    )
    all_moved = exchange(other_grads, across_pair)
    step_rows = block.shape[0]
    same_grads, query_pad = attend_final_call(
        saved, query_t, grad_t, totals, for_other, head_dim, local
    )
    all_sum = same_grads.astype(F32) + all_moved.astype(F32)
    low = all_sum[step_rows:].astype(BF16)
    pieces = [
        exchange(low[(s - 1) * step_rows : s * step_rows], frame_pairs(s, 0))
        for s in range(1, outer)
    ]
    query_back, query_here, query_away = query_side_call(
        place, query_pad, tokens_t, head_dim, count
    )
    query_moved = exchange(query_away, across_pair)
    pieces, query_back, query_here = barrier((pieces, query_back, query_here))
    swapped = add_all(all_sum[:step_rows], pieces).astype(BF16)
    beside = exchange(swapped, outer_pairs(-1))
    mine = exchange(swapped, frame_pairs(0, 1))
    beside, mine = barrier((beside, mine))
    block_rows = 2 * local // count
    padded = round_up(block_rows, 8)
    here, away, backs = pull_call(
        place, mine, swapped, beside, windows, taps, tokens_t, rows, cols, count
    )
    query_moved, backs = barrier((query_moved, backs))
    near, far = token_call(place, query_back, backs, weights)
    moved = exchange(away, frame_pairs(0, 1))
    query_own, query_pieces = scatter_weights(query_here, query_moved, padded)
    moved, query_pieces = barrier((moved, query_pieces))
    query_sum = add_all(query_own, query_pieces)
    input_grad = (near + across(far)[:, :local].astype(F32)).astype(BF16)
    own_sum, pieces = scatter_weights(here, moved, padded)
    own_sum, tail_sum = own_sum[:padded], own_sum[padded:]
    pieces, input_grad, query_sum, own_sum, tail_sum = barrier(
        (pieces, input_grad, query_sum, own_sum, tail_sum)
    )
    weight_grad, kernel_grad = finish_call(
        query_sum, own_sum, tail_sum, pieces, block_rows, local
    )
    return input_grad.reshape(tokens.shape), weight_grad, kernel_grad.transpose(1, 0, 2)


def solution(mesh):
    in_specs = (
        P(("clips", "frames"), None, None, "heads"),
        P(("clips", "frames"), None, None, "heads"),
        P(None, None, "heads"),
        P(None, None, "heads"),
    )
    out_specs = (
        P(("clips", "frames"), None, None, "heads"),
        P("clips", "frames", "heads"),
        P("clips", None, "heads"),
    )
    return jax.shard_map(shards, mesh=mesh, in_specs=in_specs, out_specs=out_specs, check_vma=False)
```
